32 devices in a mesh: gx: 4 (over y, x), gy: 8 (over z, core).
Axes of the slice: x: 2, y: 2, z: 4, core: 2. Of those that a mesh axis runs over, the one named last changes fastest.
Arguments:
- operator_t: bfloat16 [64, 512, 2432], P('gx', 'gy'), may hold values from -0.046875 to 0.046875
- data_columns: bfloat16 [2432, 384], P(('gx', 'gy')), may hold values from -6 to 6
- noise_var: float32 [2432], P(('gx', 'gy')), may hold values from 0.05 to 0.5
- class_map: int32 [64, 512], P('gx', 'gy'), may hold values from 0 to 15
- diffusion_table: float32 [16], replicated, may hold values from 0.5 to 4
- kappa_table: float32 [16], replicated, may hold values from 0.02 to 0.3
Outputs:
- hessian_block: float32 [2432, 384], P(('gx', 'gy'))
- prior_field: float32 [64, 512, 384], P('gx', 'gy')
The draws below stay inside these ranges and needn't reach their ends.
All inputs are finite; a program needn't handle non-finite values.
Results may differ from the reference program's by a relative error of at most 0.0003.
Values may be sent and summed in bfloat16 or wider, within the bound.
A program may use at most 64 MiB of HBM per device.

```python
import math
import jax
import jax.numpy as jnp
from jax import lax

K = 384
ITERS = 8
CLASSES = 16
NDATA = 2432
NX = 64
NY = 512


def place_ends(values, key, low, largest):
    place = [jax.random.randint(jax.random.fold_in(key, axis), (), 0, length) for axis, length in enumerate(values.shape)]
    main_axis = values.shape.index(max(values.shape))
    neighbour = place[:main_axis] + [(place[main_axis] + 1) % values.shape[main_axis]] + place[main_axis + 1:]
    return values.at[tuple(place)].set(low).at[tuple(neighbour)].set(largest)


def spiked(drawn, key, source, target, parts, factor):
    owner, partner = [(jnp.arange(drawn.shape[position]) // (drawn.shape[position] // parts)).reshape([-1 if axis == position else 1 for axis in range(drawn.ndim)]) for position in (source, target)]
    chosen = jax.random.permutation(key, parts)[partner]
    strong = (owner == chosen) | (owner == (partner + parts // 2) % parts)
    return jnp.where(strong, factor * drawn, drawn)


def level_of(key, shape, shards, least, largest):
    def one(axis_at, shards_of):
        steps = jax.random.uniform(jax.random.fold_in(jax.random.fold_in(key, 6), axis_at), (shards_of,), jnp.float32, least / len(shards), largest / len(shards))
        return jnp.repeat(jnp.exp(steps), shape[axis_at] // shards_of).reshape((-1,) + (1,) * (len(shape) - axis_at - 1))

    gain = one(*shards[0])
    for cut in shards[1:]:
        gain = gain * one(*cut)
    return gain


def centred(key, shape, scale, limit, cuts=(), kind=jnp.bfloat16):
    factor_of = level_of(key, shape, cuts, -0.22, 0.18) if cuts else 1.0
    result = jax.random.normal(key, shape, jnp.float32) * scale * factor_of
    return jnp.minimum(jnp.maximum(result, -limit), limit).astype(kind)


def heavy_noise(key, extent, spread, limit, pieces, heavy, kind=jnp.bfloat16):
    values = spread * jax.random.normal(key, extent, jnp.float32)
    if pieces:
        values = values * level_of(key, extent, pieces, -0.22, 0.18)
    return jnp.clip(spiked(values, jax.random.fold_in(key, 3), *heavy), -limit, limit).astype(kind)


def setup_inputs(seed: int = 0) -> dict:
    streams_of = jax.random.split(jax.random.key(seed), 7)
    operator_t = heavy_noise(streams_of[0], (NX, NY, NDATA), (NX * NY) ** -0.5, 0.046875, ((0, 4), (1, 8)), (1, 2, 8, 2.0))
    data_columns = centred(streams_of[1], (NDATA, K), 1.0, 6.0, ((0, 32),))
    noise_var = jnp.clip(jnp.exp(math.log(0.5) - 2.3025851 * jax.random.uniform(streams_of[2], (NDATA,), jnp.float32) ** level_of(streams_of[2], (NDATA,), ((0, 32),), -0.2, 0.2)), 0.05, 0.5)
    class_map = place_ends(jax.random.randint(streams_of[3], (NX, NY), 0, CLASSES), jax.random.fold_in(streams_of[3], 1), 0, CLASSES - 1).astype(jnp.int32)
    diffusion_table = jnp.clip(jnp.exp(jax.random.uniform(streams_of[4], (CLASSES,), jnp.float32, math.log(0.5), math.log(4.0))), 0.5, 4.0)
    kappa_table = jnp.clip(jnp.exp(jax.random.uniform(streams_of[5], (CLASSES,), jnp.float32, math.log(0.02), math.log(0.3))), 0.02, 0.3)
    return {"operator_t": operator_t, "data_columns": data_columns, "noise_var": noise_var, "class_map": class_map, "diffusion_table": diffusion_table, "kappa_table": kappa_table}


def lookup(classes, entries):
    onehot = (classes[..., None] == jnp.arange(entries.shape[0], dtype=jnp.int32)).astype(jnp.float32)
    return jnp.sum(onehot * entries, axis=-1)


def edge_weights(padded):
    centre = padded[1:-1, 1:-1]
    north_w = 0.5 * (centre + padded[:-2, 1:-1])
    south_w = 0.5 * (centre + padded[2:, 1:-1])
    west_w = 0.5 * (centre + padded[1:-1, :-2])
    east_w = 0.5 * (centre + padded[1:-1, 2:])
    return north_w, south_w, west_w, east_w


def jacobi_step(source, padded, weights, divisor):
    summed = source + weights[0][..., None] * padded[:-2, 1:-1]
    summed = summed + weights[1][..., None] * padded[2:, 1:-1]
    summed = summed + weights[2][..., None] * padded[1:-1, :-2]
    summed = summed + weights[3][..., None] * padded[1:-1, 2:]
    return summed / divisor[..., None]


def reference(operator_t, data_columns, noise_var, class_map, diffusion_table, kappa_table):
    diffusion = lookup(class_map, diffusion_table)
    reaction = lookup(class_map, kappa_table)
    weights = edge_weights(jnp.pad(diffusion, 1))
    divisor = reaction + weights[0] + weights[1] + weights[2] + weights[3]
    flattened = operator_t.reshape(NX * NY, NDATA)
    source = jnp.dot(flattened, data_columns, preferred_element_type=jnp.float32).reshape(NX, NY, K)
    iterate = source / divisor[..., None]
    for repeat in range(ITERS):
        padded = jnp.pad(iterate, ((1, 1), (1, 1), (0, 0)))
        iterate = jacobi_step(source, padded, weights, divisor)
    smooth = iterate.astype(jnp.bfloat16).reshape(NX * NY, K)
    forward = lax.dot_general(flattened, smooth, (((0,), (0,)), ((), ())), preferred_element_type=jnp.float32)
    return forward + noise_var[:, None] * data_columns.astype(jnp.float32), iterate
```

```python
import functools
import jax
import jax.numpy as jnp
from jax import lax
from jax.experimental import pallas as pl
from jax.experimental.pallas import tpu as pltpu
from jax.sharding import PartitionSpec as P

ITERS = 8
MESH = pl.DeviceIdType.MESH


def up8(n):
    return -(-n // 8) * 8


class Place:
    def __init__(self, dims):
        self.Y, self.X, self.Z = dims
        gx, gy = lax.axis_index("gx"), lax.axis_index("gy")
        self.y, self.x = gx // self.X, gx % self.X
        self.z, self.core = gy // 2, gy % 2
        self.n = {"x": self.X, "y": self.Y, "z": self.Z}
        self.at = {"x": self.x, "y": self.y, "z": self.z}

    def device(self, **moved):
        c = {**self.at, "core": self.core, **moved}
        return (c["y"] * self.X + c["x"], c["z"] * 2 + c["core"])

    def ahead(self, axis, d):
        return (self.at[axis] + d) % self.n[axis]

    def peers(self):
        found = [self.device(core=1 - self.core)]
        for axis in "xyz":
            found += [self.device(**{axis: self.ahead(axis, d)}) for d in range(1, self.n[axis])]
        return found

    def barrier(self):
        ready = pltpu.get_barrier_semaphore()
        peers = self.peers()
        for peer in peers:
            pl.semaphore_signal(ready, inc=1, device_id=peer, device_id_type=MESH)
        pl.semaphore_wait(ready, len(peers))


def remote(src, dst, send, recv, device):
    return pltpu.make_async_remote_copy(
        src_ref=src, dst_ref=dst, send_sem=send, recv_sem=recv, device_id=device, device_id_type=MESH
    )


def plane(ref, axis, index):
    return ref.at[:, index] if axis == "x" else ref.at[index]


def gather_kernel(dims, mine, full, own_sem, sz, rz, s1, r1, s2, r2, ss, rs):
    here = Place(dims)
    me = here.core
    sib = here.device(core=1 - me)
    home = full.at[here.y, here.x, here.z, me]
    copy = pltpu.make_async_copy(mine, home, own_sem)
    copy.start()
    here.barrier()
    copies = []
    for d in range(1, here.Z):
        sent = remote(mine, home, sz.at[d - 1], rz.at[d - 1], here.device(z=here.ahead("z", d)))
        sent.start()
        copies.append(sent)
    copy.wait()
    for d in range(1, here.Z):
        back = full.at[here.y, here.x, here.ahead("z", -d), me]
        remote(back, back, sz.at[d - 1], rz.at[d - 1], sib).wait_recv()
    for c in (0, 1):

        @pl.when(me == c)
        def _():
            near, far = "xy"[c], "yx"[c]
            sent_here = []

            def line(index, core):
                where = {**here.at, near: index}
                return full.at[where["y"], where["x"], :, core]

            def sheet(index, core):
                return full.at[index, :, :, core] if far == "y" else full.at[:, index, :, core]

            own = line(here.at[near], c)
            for d in range(1, here.n[near]):
                sent = remote(
                    own, own, s1.at[d - 1], r1.at[d - 1], here.device(**{near: here.ahead(near, d)})
                )
                sent.start()
                sent_here.append(sent)
            count = 0
            share = remote(own, own, ss.at[count], rs.at[count], sib)
            share.start()
            sent_here.append(share)
            for d in range(1, here.n[near]):
                back = line(here.ahead(near, -d), c)
                remote(back, back, s1.at[d - 1], r1.at[d - 1], sib).wait_recv()
            own = sheet(here.at[far], c)
            for d in range(1, here.n[far]):
                sent = remote(
                    own, own, s2.at[d - 1], r2.at[d - 1], here.device(**{far: here.ahead(far, d)})
                )
                sent.start()
                sent_here.append(sent)
            for d in range(1, here.n[near]):
                count += 1
                back = line(here.ahead(near, -d), c)
                share = remote(back, back, ss.at[count], rs.at[count], sib)
                share.start()
                sent_here.append(share)
            for d in range(1, here.n[far]):
                back = sheet(here.ahead(far, -d), c)
                remote(back, back, s2.at[d - 1], r2.at[d - 1], sib).wait_recv()
                count += 1
                share = remote(back, back, ss.at[count], rs.at[count], sib)
                share.start()
                sent_here.append(share)
            near2, far2 = far, near
            got = 0

            def line2(index):
                where = {**here.at, near2: index}
                return full.at[where["y"], where["x"], :, 1 - c]

            def sheet2(index):
                return full.at[index, :, :, 1 - c] if far2 == "y" else full.at[:, index, :, 1 - c]

            for d in range(0, here.n[near2]):
                back = line2(here.ahead(near2, -d))
                remote(back, back, ss.at[got], rs.at[got], sib).wait_recv()
                got += 1
            for d in range(1, here.n[far2]):
                back = sheet2(here.ahead(far2, -d))
                remote(back, back, ss.at[got], rs.at[got], sib).wait_recv()
                got += 1
            for sent in sent_here:
                sent.wait_send()

    for sent in copies:
        sent.wait_send()


def gather(dims, block):
    Y, X, Z = dims
    dma = pltpu.SemaphoreType.DMA
    widest = max(X, Y)
    return pl.pallas_call(
        functools.partial(gather_kernel, dims),
        out_shape=jax.ShapeDtypeStruct((Y, X, Z, 2) + block.shape, block.dtype),
        in_specs=[pl.BlockSpec(memory_space=pltpu.VMEM)],
        out_specs=pl.BlockSpec(memory_space=pltpu.VMEM),
        scratch_shapes=[dma]
        + [dma((max(Z - 1, 1),))] * 2
        + [dma((widest,))] * 4
        + [dma((X + Y,))] * 2,
        compiler_params=pltpu.CompilerParams(
            collective_id=0, has_side_effects=True, vmem_limit_bytes=16 << 20
        ),
    )(block)


def scatter_kernel(dims, starts, H, part, out, total, r0, r1x, r1y, r2x, r2y, r3, *sems):
    here = Place(dims)
    me = here.core
    sib = here.device(core=1 - me)
    s0, g0, s1, g1, s2, g2, s3, g3 = sems
    here.barrier()
    for c in (0, 1):

        @pl.when(me == c)
        def _():
            near, far = "xy"[c], "yx"[c]
            r1, r2 = (r1x, r2y) if c == 0 else (r1y, r2x)
            n1, n2 = here.n[near], here.n[far]
            sent_here = []
            for order, d in enumerate([*range(1, n2), 0]):
                index = here.ahead(far, d)
                sent = remote(
                    plane(part, far, index).at[:, :, pl.ds(starts[1 - c], H), :],
                    plane(r0, far, index),
                    s0.at[order],
                    g0.at[order],
                    sib,
                )
                sent.start()
                sent_here.append(sent)
            for order, d in enumerate([*range(1, n1), 0]):
                index = here.ahead(near, d)
                arrived = plane(r0, near, index)
                remote(arrived, arrived, s0.at[order], g0.at[order], sib).wait_recv()
                held = plane(total, near, index)
                held[...] = (
                    plane(part, near, index).at[:, :, pl.ds(starts[c], H), :][...] + arrived[...]
                )
                if d:
                    sent = remote(
                        held, r1.at[d - 1], s1.at[d - 1], g1.at[d - 1], here.device(**{near: index})
                    )
                    sent.start()
                    sent_here.append(sent)
            for d in range(1, n1):
                remote(r1.at[d - 1], r1.at[d - 1], s1.at[d - 1], g1.at[d - 1], sib).wait_recv()
            mine = plane(total, near, here.at[near])
            for d in [*range(1, n2), 0]:
                index = here.ahead(far, d)
                held = mine.at[index]
                value = held[...]
                for e in range(1, n1):
                    value = value + r1.at[e - 1, index][...]
                held[...] = value
                if d:
                    sent = remote(
                        held, r2.at[d - 1], s2.at[d - 1], g2.at[d - 1], here.device(**{far: index})
                    )
                    sent.start()
                    sent_here.append(sent)
            for d in range(1, n2):
                remote(r2.at[d - 1], r2.at[d - 1], s2.at[d - 1], g2.at[d - 1], sib).wait_recv()
            for d in [*range(1, here.Z), 0]:
                index = here.ahead("z", d)
                held = total.at[here.y, here.x, index]
                value = held[...]
                for e in range(1, n2):
                    value = value + r2.at[e - 1, index][...]
                held[...] = value
                if d:
                    sent = remote(
                        held, r3.at[d - 1], s3.at[d - 1], g3.at[d - 1], here.device(z=index)
                    )
                    sent.start()
                    sent_here.append(sent)
            value = total.at[here.y, here.x, here.z][...]
            for d in range(1, here.Z):
                remote(r3.at[d - 1], r3.at[d - 1], s3.at[d - 1], g3.at[d - 1], sib).wait_recv()
                value = value + r3.at[d - 1][...]
            out[...] = value
            for sent in sent_here:
                sent.wait_send()


def scatter(dims, part, rows):
    Y, X, Z = dims
    columns = part.shape[1]
    start = rows // 8 * 8
    H = max(up8(rows), up8(2 * rows) - start)
    pair = max(H + start, 2 * rows)
    part = part.reshape(Y, X, Z, 2 * rows, columns)
    if pair != 2 * rows:
        part = jnp.pad(part, ((0, 0),) * 3 + ((0, pair - 2 * rows), (0, 0)))
    dma = pltpu.SemaphoreType.DMA
    widest = max(X, Y)
    f32 = jnp.float32

    def held(*lead):
        return pltpu.VMEM(tuple(max(n, 1) for n in lead) + (H, columns), f32)

    out = pl.pallas_call(
        functools.partial(scatter_kernel, dims, (0, start), H),
        out_shape=jax.ShapeDtypeStruct((H, columns), f32),
        in_specs=[pl.BlockSpec(memory_space=pltpu.VMEM)],
        out_specs=pl.BlockSpec(memory_space=pltpu.VMEM),
        scratch_shapes=[
            held(Y, X, Z),
            held(Y, X, Z),
            held(X - 1, Y, Z),
            held(Y - 1, X, Z),
            held(X - 1, Z),
            held(Y - 1, Z),
            held(Z - 1),
        ]
        + [dma((widest,))] * 6
        + [dma((max(Z - 1, 1),))] * 2,
        compiler_params=pltpu.CompilerParams(
            collective_id=1, has_side_effects=True, vmem_limit_bytes=32 << 20
        ),
    )(part)
    core = lax.axis_index("gy") % 2
    return jnp.where(core == 0, out[:rows], out[rows - start : 2 * rows - start])


def mesh_dims():
    gx, gy = lax.axis_size("gx"), lax.axis_size("gy")
    return (gx // 2, 2, gy // 2)


def padded_2(block, sides, width):
    for axis, dim in sides:
        count = lax.axis_size(axis)
        forward = [(i, i + 1) for i in range(count - 1)]
        backward = [(target, source) for source, target in forward]
        low = lax.ppermute(
            lax.slice_in_dim(block, block.shape[dim] - width, None, axis=dim), axis, forward
        )
        high = lax.ppermute(lax.slice_in_dim(block, 0, width, axis=dim), axis, backward)
        block = jnp.concatenate([low, block, high], axis=dim)
    return block


def lookup(classes, entries):
    onehot = (classes[..., None] == jnp.arange(entries.shape[0], dtype=jnp.int32)).astype(
        jnp.float32
    )
    return jnp.sum(onehot * entries, axis=-1)


def edge_weights(padded):
    centre = padded[1:-1, 1:-1]
    north_w = 0.5 * (centre + padded[:-2, 1:-1])
    south_w = 0.5 * (centre + padded[2:, 1:-1])
    west_w = 0.5 * (centre + padded[1:-1, :-2])
    east_w = 0.5 * (centre + padded[1:-1, 2:])
    return (north_w, south_w, west_w, east_w)


def jacobi_step(source, padded, weights, divisor):
    summed = source + weights[0][..., None] * padded[:-2, 1:-1]
    summed = summed + weights[1][..., None] * padded[2:, 1:-1]
    summed = summed + weights[2][..., None] * padded[1:-1, :-2]
    summed = summed + weights[3][..., None] * padded[1:-1, 2:]
    return summed / divisor[..., None]


def local(operator_t, data_columns, noise_var, class_map, diffusion_table, kappa_table):
    tile_rows, tile_cols, data_rows = operator_t.shape
    columns_count = data_columns.shape[1]
    flattened = operator_t.reshape(tile_rows * tile_cols, data_rows)
    selected = flattened
    source = jnp.dot(
        selected,
        gather(mesh_dims(), data_columns).reshape(data_rows, columns_count),
        preferred_element_type=jnp.float32,
    )
    source = source.reshape(tile_rows, tile_cols, columns_count)
    diffusion = lookup(class_map, diffusion_table)
    reaction = lookup(class_map, kappa_table)
    margin = ITERS
    stacked = padded_2(jnp.stack([diffusion, reaction]), (("gx", 1), ("gy", 2)), margin + 1)
    weights = edge_weights(stacked[0])
    reaction_ext = stacked[1, 1:-1, 1:-1]
    extended = padded_2(source, (("gx", 0), ("gy", 1)), margin)
    global_rows = (
        lax.axis_index("gx") * tile_rows
        + jnp.arange(tile_rows + 2 * margin, dtype=jnp.int32)
        - margin
    )
    global_cols = (
        lax.axis_index("gy") * tile_cols
        + jnp.arange(tile_cols + 2 * margin, dtype=jnp.int32)
        - margin
    )
    rows_inside = (global_rows >= 0) & (global_rows < tile_rows * lax.axis_size("gx"))
    cols_inside = (global_cols >= 0) & (global_cols < tile_cols * lax.axis_size("gy"))
    inside = rows_inside[:, None] & cols_inside[None, :]
    divisor = jnp.where(
        inside, reaction_ext + weights[0] + weights[1] + weights[2] + weights[3], 1.0
    )
    retained = inside.astype(jnp.float32)[..., None]
    iterate = extended / divisor[..., None] * retained
    for repeat in range(ITERS):
        padded = jnp.pad(iterate, ((1, 1), (1, 1), (0, 0)))
        iterate = jacobi_step(extended, padded, weights, divisor) * retained
    iterate = iterate[margin : margin + tile_rows, margin : margin + tile_cols]
    smooth = iterate.astype(jnp.bfloat16).reshape(tile_rows * tile_cols, columns_count)
    selected = flattened
    partial = lax.dot_general(
        selected, smooth, (((0,), (0,)), ((), ())), preferred_element_type=jnp.float32
    )
    forward = scatter(mesh_dims(), partial, data_columns.shape[0])
    return (forward + noise_var[:, None] * data_columns.astype(jnp.float32), iterate)


def solution(mesh):
    placed = (P("gx", "gy", None), P(("gx", "gy"), None), P(("gx", "gy")), P("gx", "gy"), P(), P())
    return jax.shard_map(
        local,
        mesh=mesh,
        in_specs=placed,
        out_specs=(P(("gx", "gy"), None), P("gx", "gy", None)),
        check_vma=False,
    )
```

```python
import functools
import jax
import jax.numpy as jnp
from jax import lax
from jax.experimental import pallas as pl
from jax.experimental.pallas import tpu as pltpu
from jax.sharding import PartitionSpec as P

ITERS = 8
MESH = pl.DeviceIdType.MESH


def up8(n):
    return -(-n // 8) * 8


class Place:
    def __init__(self, dims):
        self.Y, self.X, self.Z = dims
        gx, gy = lax.axis_index("gx"), lax.axis_index("gy")
        self.y, self.x = gx // self.X, gx % self.X
        self.z, self.core = gy // 2, gy % 2
        self.n = {"x": self.X, "y": self.Y, "z": self.Z}
        self.at = {"x": self.x, "y": self.y, "z": self.z}

    def device(self, **moved):
        c = {**self.at, "core": self.core, **moved}
        return (c["y"] * self.X + c["x"], c["z"] * 2 + c["core"])

    def ahead(self, axis, d):
        return (self.at[axis] + d) % self.n[axis]

    def peers(self):
        found = [self.device(core=1 - self.core)]
        for axis in "xyz":
            found += [self.device(**{axis: self.ahead(axis, d)}) for d in range(1, self.n[axis])]
        return found

    def barrier(self):
        ready = pltpu.get_barrier_semaphore()
        peers = self.peers()
        for peer in peers:
            pl.semaphore_signal(ready, inc=1, device_id=peer, device_id_type=MESH)
        pl.semaphore_wait(ready, len(peers))


def remote(src, dst, send, recv, device):
    return pltpu.make_async_remote_copy(
        src_ref=src, dst_ref=dst, send_sem=send, recv_sem=recv, device_id=device, device_id_type=MESH
    )


def plane(ref, axis, index):
    return ref.at[:, index] if axis == "x" else ref.at[index]


def gather_kernel(dims, mine, full, own_sem, sz, rz, s1, r1, s2, r2, ss, rs):
    here = Place(dims)
    me = here.core
    sib = here.device(core=1 - me)
    home = full.at[here.y, here.x, here.z, me]
    copy = pltpu.make_async_copy(mine, home, own_sem)
    copy.start()
    here.barrier()
    copies = []
    for d in range(1, here.Z):
        sent = remote(mine, home, sz.at[d - 1], rz.at[d - 1], here.device(z=here.ahead("z", d)))
        sent.start()
        copies.append(sent)
    copy.wait()
    for d in range(1, here.Z):
        back = full.at[here.y, here.x, here.ahead("z", -d), me]
        remote(back, back, sz.at[d - 1], rz.at[d - 1], sib).wait_recv()
    for c in (0, 1):

        @pl.when(me == c)
        def _():
            near, far = "xy"[c], "yx"[c]
            sent_here = []

            def line(index, core):
                where = {**here.at, near: index}
                return full.at[where["y"], where["x"], :, core]

            def sheet(index, core):
                return full.at[index, :, :, core] if far == "y" else full.at[:, index, :, core]

            own = line(here.at[near], c)
            for d in range(1, here.n[near]):
                sent = remote(
                    own, own, s1.at[d - 1], r1.at[d - 1], here.device(**{near: here.ahead(near, d)})
                )
                sent.start()
                sent_here.append(sent)
            count = 0
            share = remote(own, own, ss.at[count], rs.at[count], sib)
            share.start()
            sent_here.append(share)
            for d in range(1, here.n[near]):
                back = line(here.ahead(near, -d), c)
                remote(back, back, s1.at[d - 1], r1.at[d - 1], sib).wait_recv()
            own = sheet(here.at[far], c)
            for d in range(1, here.n[far]):
                sent = remote(
                    own, own, s2.at[d - 1], r2.at[d - 1], here.device(**{far: here.ahead(far, d)})
                )
                sent.start()
                sent_here.append(sent)
            for d in range(1, here.n[near]):
                count += 1
                back = line(here.ahead(near, -d), c)
                share = remote(back, back, ss.at[count], rs.at[count], sib)
                share.start()
                sent_here.append(share)
            for d in range(1, here.n[far]):
                back = sheet(here.ahead(far, -d), c)
                remote(back, back, s2.at[d - 1], r2.at[d - 1], sib).wait_recv()
                count += 1
                share = remote(back, back, ss.at[count], rs.at[count], sib)
                share.start()
                sent_here.append(share)
            near2, far2 = far, near
            got = 0

            def line2(index):
                where = {**here.at, near2: index}
                return full.at[where["y"], where["x"], :, 1 - c]

            def sheet2(index):
                return full.at[index, :, :, 1 - c] if far2 == "y" else full.at[:, index, :, 1 - c]

            for d in range(0, here.n[near2]):
                back = line2(here.ahead(near2, -d))
                remote(back, back, ss.at[got], rs.at[got], sib).wait_recv()
                got += 1
            for d in range(1, here.n[far2]):
                back = sheet2(here.ahead(far2, -d))
                remote(back, back, ss.at[got], rs.at[got], sib).wait_recv()
                got += 1
            for sent in sent_here:
                sent.wait_send()

    for sent in copies:
        sent.wait_send()


def gather(dims, block):
    Y, X, Z = dims
    dma = pltpu.SemaphoreType.DMA
    widest = max(X, Y)
    return pl.pallas_call(
        functools.partial(gather_kernel, dims),
        out_shape=jax.ShapeDtypeStruct((Y, X, Z, 2) + block.shape, block.dtype),
        in_specs=[pl.BlockSpec(memory_space=pltpu.VMEM)],
        out_specs=pl.BlockSpec(memory_space=pltpu.VMEM),
        scratch_shapes=[dma]
        + [dma((max(Z - 1, 1),))] * 2
        + [dma((widest,))] * 4
        + [dma((X + Y,))] * 2,
        compiler_params=pltpu.CompilerParams(
            collective_id=0, has_side_effects=True, vmem_limit_bytes=16 << 20
        ),
    )(block)


def scatter_kernel(dims, starts, H, part, out, total, r0, r1x, r1y, r2x, r2y, r3, *sems):
    here = Place(dims)
    me = here.core
    sib = here.device(core=1 - me)
    s0, g0, s1, g1, s2, g2, s3, g3 = sems
    here.barrier()
    for c in (0, 1):

        @pl.when(me == c)
        def _():
            near, far = "xy"[c], "yx"[c]
            r1, r2 = (r1x, r2y) if c == 0 else (r1y, r2x)
            n1, n2 = here.n[near], here.n[far]
            sent_here = []
            for order, d in enumerate([*range(1, n2), 0]):
                index = here.ahead(far, d)
                sent = remote(
                    plane(part, far, index).at[:, :, pl.ds(starts[1 - c], H), :],
                    plane(r0, far, index),
                    s0.at[order],
                    g0.at[order],
                    sib,
                )
                sent.start()
                sent_here.append(sent)
            for order, d in enumerate([*range(1, n1), 0]):
                index = here.ahead(near, d)
                arrived = plane(r0, near, index)
                remote(arrived, arrived, s0.at[order], g0.at[order], sib).wait_recv()
                held = plane(total, near, index)
                held[...] = (
                    plane(part, near, index).at[:, :, pl.ds(starts[c], H), :][...] + arrived[...]
                )
                if d:
                    sent = remote(
                        held, r1.at[d - 1], s1.at[d - 1], g1.at[d - 1], here.device(**{near: index})
                    )
                    sent.start()
                    sent_here.append(sent)
            for d in range(1, n1):
                remote(r1.at[d - 1], r1.at[d - 1], s1.at[d - 1], g1.at[d - 1], sib).wait_recv()
            mine = plane(total, near, here.at[near])
            for d in [*range(1, n2), 0]:
                index = here.ahead(far, d)
                held = mine.at[index]
                value = held[...]
                for e in range(1, n1):
                    value = value + r1.at[e - 1, index][...]
                held[...] = value
                if d:
                    sent = remote(
                        held, r2.at[d - 1], s2.at[d - 1], g2.at[d - 1], here.device(**{far: index})
                    )
                    sent.start()
                    sent_here.append(sent)
            for d in range(1, n2):
                remote(r2.at[d - 1], r2.at[d - 1], s2.at[d - 1], g2.at[d - 1], sib).wait_recv()
            for d in [*range(1, here.Z), 0]:
                index = here.ahead("z", d)
                held = total.at[here.y, here.x, index]
                value = held[...]
                for e in range(1, n2):
                    value = value + r2.at[e - 1, index][...]
                held[...] = value
                if d:
                    sent = remote(
                        held, r3.at[d - 1], s3.at[d - 1], g3.at[d - 1], here.device(z=index)
                    )
                    sent.start()
                    sent_here.append(sent)
            value = total.at[here.y, here.x, here.z][...]
            for d in range(1, here.Z):
                remote(r3.at[d - 1], r3.at[d - 1], s3.at[d - 1], g3.at[d - 1], sib).wait_recv()
                value = value + r3.at[d - 1][...]
            out[...] = value
            for sent in sent_here:
                sent.wait_send()


def scatter(dims, part, rows):
    Y, X, Z = dims
    columns = part.shape[1]
    start = rows // 8 * 8
    H = max(up8(rows), up8(2 * rows) - start)
    pair = max(H + start, 2 * rows)
    part = part.reshape(Y, X, Z, 2 * rows, columns)
    if pair != 2 * rows:
        part = jnp.pad(part, ((0, 0),) * 3 + ((0, pair - 2 * rows), (0, 0)))
    dma = pltpu.SemaphoreType.DMA
    widest = max(X, Y)
    f32 = jnp.float32

    def held(*lead):
        return pltpu.VMEM(tuple(max(n, 1) for n in lead) + (H, columns), f32)

    out = pl.pallas_call(
        functools.partial(scatter_kernel, dims, (0, start), H),
        out_shape=jax.ShapeDtypeStruct((H, columns), f32),
        in_specs=[pl.BlockSpec(memory_space=pltpu.VMEM)],
        out_specs=pl.BlockSpec(memory_space=pltpu.VMEM),
        scratch_shapes=[
            held(Y, X, Z),
            held(Y, X, Z),
            held(X - 1, Y, Z),
            held(Y - 1, X, Z),
            held(X - 1, Z),
            held(Y - 1, Z),
            held(Z - 1),
        ]
        + [dma((widest,))] * 6
        + [dma((max(Z - 1, 1),))] * 2,
        compiler_params=pltpu.CompilerParams(
            collective_id=1, has_side_effects=True, vmem_limit_bytes=32 << 20
        ),
    )(part)
    core = lax.axis_index("gy") % 2
    return jnp.where(core == 0, out[:rows], out[rows - start : 2 * rows - start])


def smooth_kernel(
    counts, start, coef, prior, smooth, s, u, v, up_out, down_out, up_in, down_in, local, send, recv
):
    rows, cols, width = start.shape
    m = ITERS
    gx, gy = lax.axis_index("gx"), lax.axis_index("gy")
    count_x, count_y = counts
    sides = {
        "n": (gx > 0, (gx - 1, gy), gx < count_x - 1),
        "s": (gx < count_x - 1, (gx + 1, gy), gx > 0),
        "w": (gy > 0, (gx, gy - 1), gy < count_y - 1),
        "e": (gy < count_y - 1, (gx, gy + 1), gy > 0),
    }
    inner_r, inner_c = pl.ds(m, rows), pl.ds(m, cols)
    low, high_r, high_c = pl.ds(0, m), pl.ds(m + rows, m), pl.ds(m + cols, m)
    home = pltpu.make_async_copy(start, s.at[inner_r, inner_c], local)
    home.start()
    for side, where in (("n", (low, slice(None))), ("s", (high_r, slice(None)))):

        @pl.when(jnp.logical_not(sides[side][0]))
        def _():
            s[where] = jnp.zeros((m, cols + 2 * m, width), jnp.float32)

    for side, where in (("w", low), ("e", high_c)):

        @pl.when(jnp.logical_not(sides[side][0]))
        def _():
            s[:, where] = jnp.zeros((rows + 2 * m, m, width), jnp.float32)

    ready = pltpu.get_barrier_semaphore()
    for has, peer, _ in sides.values():

        @pl.when(has)
        def _():
            pl.semaphore_signal(ready, inc=1, device_id=peer, device_id_type=MESH)

    up_out[...] = start[1:m].astype(jnp.bfloat16)
    down_out[...] = start[rows - m : rows - 1].astype(jnp.bfloat16)
    pl.semaphore_wait(ready, sum(jnp.where(has, 1, 0) for has, _, _ in sides.values()))

    first = (
        (0, "n", start.at[pl.ds(0, 1)], s.at[pl.ds(m + rows, 1), inner_c]),
        (1, "s", start.at[pl.ds(rows - 1, 1)], s.at[pl.ds(m - 1, 1), inner_c]),
        (2, "n", up_out, up_in),
        (3, "s", down_out, down_in),
        (4, "w", start.at[:, pl.ds(0, m)], s.at[inner_r, high_c]),
        (5, "e", start.at[:, pl.ds(cols - m, m)], s.at[inner_r, low]),
    )
    second = (
        (6, "w", s.at[low, pl.ds(m, m)], s.at[low, high_c]),
        (7, "w", s.at[high_r, pl.ds(m, m)], s.at[high_r, high_c]),
        (8, "e", s.at[low, pl.ds(cols, m)], s.at[low, low]),
        (9, "e", s.at[high_r, pl.ds(cols, m)], s.at[high_r, low]),
    )

    def each(group, what):
        for number, side, src, dst in group:
            has, peer, gets = sides[side]
            copy = remote(src, dst, send.at[number], recv.at[number], peer)

            @pl.when(gets if what == "wait_recv" else has)
            def _():
                getattr(copy, what)()

    each(first, "start")
    home.wait()
    each(first, "wait_recv")

    @pl.when(sides["s"][0])
    def _():
        s[pl.ds(m + rows + 1, m - 1), inner_c] = up_in[...].astype(jnp.float32)

    @pl.when(sides["n"][0])
    def _():
        s[pl.ds(0, m - 1), inner_c] = down_in[...].astype(jnp.float32)

    each(second, "start")
    each(second, "wait_recv")
    each(first, "wait_send")
    each(second, "wait_send")

    held = [s, u, v]
    wide = cols + 2 * m
    for step in range(1, ITERS + 1):
        old = s if step == 1 else held[1 + step % 2]
        new = held[1 + (step + 1) % 2]
        last = step == ITERS

        @pl.loop(step, rows + 2 * m - step)
        def _(r):
            for g in range(width // 128):
                lanes = pl.ds(g * 128, 128)
                centre = old[r, :, lanes]
                value = s[r, :, lanes] + coef[0, r] * old[r - 1, :, lanes]
                value = value + coef[1, r] * old[r + 1, :, lanes]
                value = value + coef[2, r] * pltpu.roll(centre, 1, 0)
                value = value + coef[3, r] * pltpu.roll(centre, wide - 1, 0)
                if last:
                    prior[r - m, :, lanes] = value[m : m + cols]
                    smooth[r - m, :, lanes] = value[m : m + cols].astype(jnp.bfloat16)
                else:
                    new[r, :, lanes] = value


def smoothed(start, coef):
    rows, cols, width = start.shape
    m = ITERS
    whole = pltpu.VMEM((rows + 2 * m, cols + 2 * m, width), jnp.float32)
    strip = pltpu.VMEM((m - 1, cols, width), jnp.bfloat16)
    dma = pltpu.SemaphoreType.DMA
    vmem = pl.BlockSpec(memory_space=pltpu.VMEM)
    return pl.pallas_call(
        functools.partial(smooth_kernel, (lax.axis_size("gx"), lax.axis_size("gy"))),
        out_shape=(
            jax.ShapeDtypeStruct(start.shape, jnp.float32),
            jax.ShapeDtypeStruct(start.shape, jnp.bfloat16),
        ),
        in_specs=[vmem, vmem],
        out_specs=(vmem, vmem),
        scratch_shapes=[whole] * 3 + [strip] * 4 + [dma, dma((10,)), dma((10,))],
        compiler_params=pltpu.CompilerParams(
            collective_id=2, has_side_effects=True, vmem_limit_bytes=40 << 20
        ),
    )(start, coef)


def mesh_dims():
    gx, gy = lax.axis_size("gx"), lax.axis_size("gy")
    return (gx // 2, 2, gy // 2)


def lookup(classes, entries):
    onehot = (classes[..., None] == jnp.arange(entries.shape[0], dtype=jnp.int32)).astype(
        jnp.float32
    )
    return jnp.sum(onehot * entries, axis=-1)


def edge_weights(padded):
    centre = padded[1:-1, 1:-1]
    north_w = 0.5 * (centre + padded[:-2, 1:-1])
    south_w = 0.5 * (centre + padded[2:, 1:-1])
    west_w = 0.5 * (centre + padded[1:-1, :-2])
    east_w = 0.5 * (centre + padded[1:-1, 2:])
    return (north_w, south_w, west_w, east_w)


def local(operator_t, data_columns, noise_var, class_map, diffusion_table, kappa_table):
    tile_rows, tile_cols, data_rows = operator_t.shape
    count, width = data_columns.shape
    gx_size, gy_size = lax.axis_size("gx"), lax.axis_size("gy")
    flattened = operator_t.reshape(tile_rows * tile_cols, data_rows)
    points = tile_rows * tile_cols
    extra = -(-points // width)
    classes = jnp.pad(class_map.reshape(points).astype(jnp.bfloat16), (0, extra * width - points))
    block = jnp.concatenate([data_columns, classes.reshape(extra, width)], axis=0)
    full = gather(mesh_dims(), block)
    data = full[..., :count, :].reshape(data_rows, width)
    classes = full[..., count:, :].reshape(gx_size, gy_size, extra * width)[..., :points]
    classes = classes.reshape(gx_size, gy_size, tile_rows, tile_cols).astype(jnp.int32)
    classes = classes.transpose(0, 2, 1, 3).reshape(gx_size * tile_rows, gy_size * tile_cols)
    edge = ITERS + 1
    classes = jnp.pad(classes, edge, constant_values=-1)
    window = lax.dynamic_slice(
        classes,
        (lax.axis_index("gx") * tile_rows, lax.axis_index("gy") * tile_cols),
        (tile_rows + 2 * edge, tile_cols + 2 * edge),
    )
    inside = (window >= 0)[1:-1, 1:-1]
    weights = edge_weights(lookup(window, diffusion_table))
    reaction = lookup(window, kappa_table)[1:-1, 1:-1]
    divisor = jnp.where(inside, reaction + weights[0] + weights[1] + weights[2] + weights[3], 1.0)
    coef = jnp.stack([jnp.where(inside, w / divisor, 0.0) for w in weights])
    coef = jnp.broadcast_to(coef[..., None], coef.shape + (128,))
    source = jnp.dot(flattened, data, preferred_element_type=jnp.float32)
    tile_divisor = divisor[ITERS:-ITERS, ITERS:-ITERS]
    start = source.reshape(tile_rows, tile_cols, width) / tile_divisor[..., None]
    iterate, smooth = smoothed(start, coef)
    partial = lax.dot_general(
        flattened,
        smooth.reshape(points, width),
        (((0,), (0,)), ((), ())),
        preferred_element_type=jnp.float32,
    )
    forward = scatter(mesh_dims(), partial, count)
    return (forward + noise_var[:, None] * data_columns.astype(jnp.float32), iterate)


def solution(mesh):
    placed = (P("gx", "gy", None), P(("gx", "gy"), None), P(("gx", "gy")), P("gx", "gy"), P(), P())
    return jax.shard_map(
        local,
        mesh=mesh,
        in_specs=placed,
        out_specs=(P(("gx", "gy"), None), P("gx", "gy", None)),
        check_vma=False,
    )
```

```python
import functools
import jax
import jax.numpy as jnp
from jax import lax
from jax.experimental import pallas as pl
from jax.experimental.pallas import tpu as pltpu
from jax.sharding import PartitionSpec as P

ITERS = 8
MESH = pl.DeviceIdType.MESH


def up8(n):
    return -(-n // 8) * 8


class Place:
    def __init__(self, dims):
        self.Y, self.X, self.Z = dims
        gx, gy = lax.axis_index("gx"), lax.axis_index("gy")
        self.y, self.x = gx // self.X, gx % self.X
        self.z, self.core = gy // 2, gy % 2
        self.n = {"x": self.X, "y": self.Y, "z": self.Z}
        self.at = {"x": self.x, "y": self.y, "z": self.z}

    def device(self, **moved):
        c = {**self.at, "core": self.core, **moved}
        return (c["y"] * self.X + c["x"], c["z"] * 2 + c["core"])

    def ahead(self, axis, d):
        return (self.at[axis] + d) % self.n[axis]

    def peers(self):
        found = [self.device(core=1 - self.core)]
        for axis in "xyz":
            found += [self.device(**{axis: self.ahead(axis, d)}) for d in range(1, self.n[axis])]
        return found

    def barrier(self):
        ready = pltpu.get_barrier_semaphore()
        peers = self.peers()
        for peer in peers:
            pl.semaphore_signal(ready, inc=1, device_id=peer, device_id_type=MESH)
        pl.semaphore_wait(ready, len(peers))


def remote(src, dst, send, recv, device):
    return pltpu.make_async_remote_copy(
        src_ref=src, dst_ref=dst, send_sem=send, recv_sem=recv, device_id=device, device_id_type=MESH
    )


def gather_kernel(dims, mine, full, own_sem, sz, rz, s1, r1, s2, r2, ss, rs):
    here = Place(dims)
    me = here.core
    sib = here.device(core=1 - me)
    home = full.at[here.y, here.x, here.z, me]
    copy = pltpu.make_async_copy(mine, home, own_sem)
    copy.start()
    here.barrier()
    copies = []
    for d in range(1, here.Z):
        sent = remote(mine, home, sz.at[d - 1], rz.at[d - 1], here.device(z=here.ahead("z", d)))
        sent.start()
        copies.append(sent)
    copy.wait()
    for d in range(1, here.Z):
        back = full.at[here.y, here.x, here.ahead("z", -d), me]
        remote(back, back, sz.at[d - 1], rz.at[d - 1], sib).wait_recv()
    for c in (0, 1):

        @pl.when(me == c)
        def _():
            near, far = "xy"[c], "yx"[c]
            sent_here = []

            def line(index, core):
                where = {**here.at, near: index}
                return full.at[where["y"], where["x"], :, core]

            def sheet(index, core):
                return full.at[index, :, :, core] if far == "y" else full.at[:, index, :, core]

            own = line(here.at[near], c)
            for d in range(1, here.n[near]):
                sent = remote(
                    own, own, s1.at[d - 1], r1.at[d - 1], here.device(**{near: here.ahead(near, d)})
                )
                sent.start()
                sent_here.append(sent)
            count = 0
            share = remote(own, own, ss.at[count], rs.at[count], sib)
            share.start()
            sent_here.append(share)
            for d in range(1, here.n[near]):
                back = line(here.ahead(near, -d), c)
                remote(back, back, s1.at[d - 1], r1.at[d - 1], sib).wait_recv()
            own = sheet(here.at[far], c)
            for d in range(1, here.n[far]):
                sent = remote(
                    own, own, s2.at[d - 1], r2.at[d - 1], here.device(**{far: here.ahead(far, d)})
                )
                sent.start()
                sent_here.append(sent)
            for d in range(1, here.n[near]):
                count += 1
                back = line(here.ahead(near, -d), c)
                share = remote(back, back, ss.at[count], rs.at[count], sib)
                share.start()
                sent_here.append(share)
            for d in range(1, here.n[far]):
                back = sheet(here.ahead(far, -d), c)
                remote(back, back, s2.at[d - 1], r2.at[d - 1], sib).wait_recv()
                count += 1
                share = remote(back, back, ss.at[count], rs.at[count], sib)
                share.start()
                sent_here.append(share)
            near2, far2 = far, near
            got = 0

            def line2(index):
                where = {**here.at, near2: index}
                return full.at[where["y"], where["x"], :, 1 - c]

            def sheet2(index):
                return full.at[index, :, :, 1 - c] if far2 == "y" else full.at[:, index, :, 1 - c]

            for d in range(0, here.n[near2]):
                back = line2(here.ahead(near2, -d))
                remote(back, back, ss.at[got], rs.at[got], sib).wait_recv()
                got += 1
            for d in range(1, here.n[far2]):
                back = sheet2(here.ahead(far2, -d))
                remote(back, back, ss.at[got], rs.at[got], sib).wait_recv()
                got += 1
            for sent in sent_here:
                sent.wait_send()

    for sent in copies:
        sent.wait_send()


def gather(dims, block):
    Y, X, Z = dims
    dma = pltpu.SemaphoreType.DMA
    widest = max(X, Y)
    return pl.pallas_call(
        functools.partial(gather_kernel, dims),
        out_shape=jax.ShapeDtypeStruct((Y, X, Z, 2) + block.shape, block.dtype),
        in_specs=[pl.BlockSpec(memory_space=pltpu.VMEM)],
        out_specs=pl.BlockSpec(memory_space=pltpu.VMEM),
        scratch_shapes=[dma]
        + [dma((max(Z - 1, 1),))] * 2
        + [dma((widest,))] * 4
        + [dma((X + Y,))] * 2,
        compiler_params=pltpu.CompilerParams(
            collective_id=0, has_side_effects=True, vmem_limit_bytes=16 << 20
        ),
    )(block)


def scatter_kernel(dims, starts, H, fused, *refs):
    if fused:
        operator, field, out, total, r0, r1x, r1y, r2x, r2y, r3, part, wide, *sems = refs
    else:
        part, out, total, r0, r1x, r1y, r2x, r2y, r3, *sems = refs
    here = Place(dims)
    Y, X, Z = dims
    pair = part.shape[3]
    me = here.core
    sib = here.device(core=1 - me)
    s0, g0, s1, g1, s2, g2, s3, g3 = sems
    ready = pltpu.get_barrier_semaphore()
    peers = here.peers()
    for peer in peers:
        pl.semaphore_signal(ready, inc=1, device_id=peer, device_id_type=MESH)
    order = [(dy, dx) for dy in [*range(1, Y), 0] for dx in [*range(1, X), 0]]
    order.sort(key=lambda step: (step[0] == 0) + (step[1] == 0))
    for number, (dy, dx) in enumerate(order):
        y, x = here.ahead("y", dy), here.ahead("x", dx)
        if fused:
            span = wide.shape[0]
            row = (y * X + x) * (Z * pair)
            base = jnp.minimum(row // 128, (operator.shape[1] - span) // 128) * 128
            wide[...] = lax.dot_general(
                operator[:, pl.ds(pl.multiple_of(base, 128), span)],
                field[...],
                (((0,), (0,)), ((), ())),
                preferred_element_type=jnp.float32,
            )
            for z in range(Z):
                part[y, x, z] = wide[pl.ds(pl.multiple_of(row - base + z * pair, 8), pair), :]
        if number == 0:
            pl.semaphore_wait(ready, len(peers))
        for c in (0, 1):

            @pl.when(me == c)
            def _():
                remote(
                    part.at[y, x, :, pl.ds(starts[1 - c], H), :],
                    r0.at[y, x],
                    s0.at[number],
                    g0.at[number],
                    sib,
                ).start()

    for c in (0, 1):

        @pl.when(me == c)
        def _():
            near, far = "xy"[c], "yx"[c]
            r1, r2 = (r1x, r2y) if c == 0 else (r1y, r2x)
            n1, n2 = here.n[near], here.n[far]
            sent_here = []
            sorted_steps = sorted(
                enumerate(order), key=lambda item: (item[1][1 - c] == 0, item[0])
            )
            for number, (dy, dx) in sorted_steps:
                y, x = here.ahead("y", dy), here.ahead("x", dx)
                arrived = r0.at[y, x]
                remote(arrived, arrived, s0.at[number], g0.at[number], sib).wait_recv()
                held = total.at[y, x]
                held[...] = part[y, x, :, pl.ds(starts[c], H), :] + arrived[...]
                d = (dx, dy)[c]
                if d:
                    sent = remote(
                        held,
                        r1.at[d - 1, (y, x)[c]],
                        s1.at[number],
                        g1.at[number],
                        here.device(**{near: (x, y)[c]}),
                    )
                    sent.start()
                    sent_here.append(sent)
            for d2 in [*range(1, n2), 0]:
                index = here.ahead(far, d2)
                held = total.at[(index, here.x) if c == 0 else (here.y, index)]
                value = held[...]
                for d in range(1, n1):
                    number = order.index((d2, d) if c == 0 else (d, d2))
                    back = r1.at[d - 1, index]
                    remote(back, back, s1.at[number], g1.at[number], sib).wait_recv()
                    value = value + back[...]
                held[...] = value
                if d2:
                    sent = remote(
                        held, r2.at[d2 - 1], s2.at[d2 - 1], g2.at[d2 - 1],
                        here.device(**{far: index}),
                    )
                    sent.start()
                    sent_here.append(sent)
            for d in range(1, n2):
                remote(r2.at[d - 1], r2.at[d - 1], s2.at[d - 1], g2.at[d - 1], sib).wait_recv()
            for d in [*range(1, Z), 0]:
                index = here.ahead("z", d)
                held = total.at[here.y, here.x, index]
                value = held[...]
                for e in range(1, n2):
                    value = value + r2.at[e - 1, index][...]
                held[...] = value
                if d:
                    sent = remote(
                        held, r3.at[d - 1], s3.at[d - 1], g3.at[d - 1], here.device(z=index)
                    )
                    sent.start()
                    sent_here.append(sent)
            value = total.at[here.y, here.x, here.z][...]
            for d in range(1, Z):
                remote(r3.at[d - 1], r3.at[d - 1], s3.at[d - 1], g3.at[d - 1], sib).wait_recv()
                value = value + r3.at[d - 1][...]
            out[...] = value
            for sent in sent_here:
                sent.wait_send()
            for number, (dy, dx) in enumerate(order):
                y, x = here.ahead("y", dy), here.ahead("x", dx)
                remote(
                    part.at[y, x, :, pl.ds(starts[1 - c], H), :],
                    r0.at[y, x],
                    s0.at[number],
                    g0.at[number],
                    sib,
                ).wait_send()


def scatter(dims, operator, field, rows):
    Y, X, Z = dims
    points, data_rows = operator.shape
    columns = field.shape[1]
    start = rows // 8 * 8
    H = max(up8(rows), up8(2 * rows) - start)
    pair = max(H + start, 2 * rows)
    group = Z * pair
    span = -(-(group + 127) // 128) * 128
    fused = pair == 2 * rows and pair % 8 == 0 and data_rows % 128 == 0 and span <= data_rows
    dma = pltpu.SemaphoreType.DMA
    widest = max(X, Y)
    f32 = jnp.float32

    def held(*lead):
        return pltpu.VMEM(tuple(max(n, 1) for n in lead) + (H, columns), f32)

    scratch = [
        held(Y, X, Z),
        held(Y, X, Z),
        held(X - 1, Y, Z),
        held(Y - 1, X, Z),
        held(X - 1, Z),
        held(Y - 1, Z),
        held(Z - 1),
    ]
    if fused:
        given = (operator, field)
        scratch += [pltpu.VMEM((Y, X, Z, pair, columns), f32), pltpu.VMEM((span, columns), f32)]
    else:
        part = lax.dot_general(
            operator, field, (((0,), (0,)), ((), ())), preferred_element_type=f32
        ).reshape(Y, X, Z, 2 * rows, columns)
        given = (jnp.pad(part, ((0, 0),) * 3 + ((0, pair - 2 * rows), (0, 0))),)
    vmem = pl.BlockSpec(memory_space=pltpu.VMEM)
    out = pl.pallas_call(
        functools.partial(scatter_kernel, dims, (0, start), H, fused),
        out_shape=jax.ShapeDtypeStruct((H, columns), f32),
        in_specs=[vmem] * len(given),
        out_specs=vmem,
        scratch_shapes=scratch
        + [dma((X * Y,))] * 4
        + [dma((widest,))] * 2
        + [dma((max(Z - 1, 1),))] * 2,
        compiler_params=pltpu.CompilerParams(
            collective_id=1, has_side_effects=True, vmem_limit_bytes=40 << 20
        ),
    )(*given)
    core = lax.axis_index("gy") % 2
    return jnp.where(core == 0, out[:rows], out[rows - start : 2 * rows - start])


def smooth_kernel(
    counts, start, coef, prior, smooth, s, u, v, up_out, down_out, up_in, down_in, local, send, recv
):
    rows, cols, width = start.shape
    m = ITERS
    gx, gy = lax.axis_index("gx"), lax.axis_index("gy")
    count_x, count_y = counts
    sides = {
        "n": (gx > 0, (gx - 1, gy), gx < count_x - 1),
        "s": (gx < count_x - 1, (gx + 1, gy), gx > 0),
        "w": (gy > 0, (gx, gy - 1), gy < count_y - 1),
        "e": (gy < count_y - 1, (gx, gy + 1), gy > 0),
    }
    inner_r, inner_c = pl.ds(m, rows), pl.ds(m, cols)
    low, high_r, high_c = pl.ds(0, m), pl.ds(m + rows, m), pl.ds(m + cols, m)
    home = pltpu.make_async_copy(start, s.at[inner_r, inner_c], local)
    home.start()
    for side, where in (("n", (low, slice(None))), ("s", (high_r, slice(None)))):

        @pl.when(jnp.logical_not(sides[side][0]))
        def _():
            s[where] = jnp.zeros((m, cols + 2 * m, width), jnp.float32)

    for side, where in (("w", low), ("e", high_c)):

        @pl.when(jnp.logical_not(sides[side][0]))
        def _():
            s[:, where] = jnp.zeros((rows + 2 * m, m, width), jnp.float32)

    ready = pltpu.get_barrier_semaphore()
    for has, peer, _ in sides.values():

        @pl.when(has)
        def _():
            pl.semaphore_signal(ready, inc=1, device_id=peer, device_id_type=MESH)

    up_out[...] = start[1:m].astype(jnp.bfloat16)
    down_out[...] = start[rows - m : rows - 1].astype(jnp.bfloat16)
    pl.semaphore_wait(ready, sum(jnp.where(has, 1, 0) for has, _, _ in sides.values()))

    first = (
        (0, "n", start.at[pl.ds(0, 1)], s.at[pl.ds(m + rows, 1), inner_c]),
        (1, "s", start.at[pl.ds(rows - 1, 1)], s.at[pl.ds(m - 1, 1), inner_c]),
        (2, "n", up_out, up_in),
        (3, "s", down_out, down_in),
        (4, "w", start.at[:, pl.ds(0, m)], s.at[inner_r, high_c]),
        (5, "e", start.at[:, pl.ds(cols - m, m)], s.at[inner_r, low]),
    )
    second = (
        (6, "w", s.at[low, pl.ds(m, m)], s.at[low, high_c]),
        (7, "w", s.at[high_r, pl.ds(m, m)], s.at[high_r, high_c]),
        (8, "e", s.at[low, pl.ds(cols, m)], s.at[low, low]),
        (9, "e", s.at[high_r, pl.ds(cols, m)], s.at[high_r, low]),
    )

    def each(group, what):
        for number, side, src, dst in group:
            has, peer, gets = sides[side]
            copy = remote(src, dst, send.at[number], recv.at[number], peer)

            @pl.when(gets if what == "wait_recv" else has)
            def _():
                getattr(copy, what)()

    each(first, "start")
    home.wait()
    each(first, "wait_recv")

    @pl.when(sides["s"][0])
    def _():
        s[pl.ds(m + rows + 1, m - 1), inner_c] = up_in[...].astype(jnp.float32)

    @pl.when(sides["n"][0])
    def _():
        s[pl.ds(0, m - 1), inner_c] = down_in[...].astype(jnp.float32)

    each(second, "start")
    each(second, "wait_recv")
    each(first, "wait_send")
    each(second, "wait_send")

    held = [s, u, v]
    wide = cols + 2 * m
    for step in range(1, ITERS + 1):
        old = s if step == 1 else held[1 + step % 2]
        new = held[1 + (step + 1) % 2]
        last = step == ITERS

        @pl.loop(step, rows + 2 * m - step)
        def _(r):
            for g in range(width // 128):
                lanes = pl.ds(g * 128, 128)
                centre = old[r, :, lanes]
                value = s[r, :, lanes] + coef[0, r] * old[r - 1, :, lanes]
                value = value + coef[1, r] * old[r + 1, :, lanes]
                value = value + coef[2, r] * pltpu.roll(centre, 1, 0)
                value = value + coef[3, r] * pltpu.roll(centre, wide - 1, 0)
                if last:
                    prior[r - m, :, lanes] = value[m : m + cols]
                    smooth[r - m, :, lanes] = value[m : m + cols].astype(jnp.bfloat16)
                else:
                    new[r, :, lanes] = value


def smoothed(start, coef):
    rows, cols, width = start.shape
    m = ITERS
    whole = pltpu.VMEM((rows + 2 * m, cols + 2 * m, width), jnp.float32)
    strip = pltpu.VMEM((m - 1, cols, width), jnp.bfloat16)
    dma = pltpu.SemaphoreType.DMA
    vmem = pl.BlockSpec(memory_space=pltpu.VMEM)
    return pl.pallas_call(
        functools.partial(smooth_kernel, (lax.axis_size("gx"), lax.axis_size("gy"))),
        out_shape=(
            jax.ShapeDtypeStruct(start.shape, jnp.float32),
            jax.ShapeDtypeStruct(start.shape, jnp.bfloat16),
        ),
        in_specs=[vmem, vmem],
        out_specs=(vmem, vmem),
        scratch_shapes=[whole] * 3 + [strip] * 4 + [dma, dma((10,)), dma((10,))],
        compiler_params=pltpu.CompilerParams(
            collective_id=2, has_side_effects=True, vmem_limit_bytes=40 << 20
        ),
    )(start, coef)


def mesh_dims():
    gx, gy = lax.axis_size("gx"), lax.axis_size("gy")
    return (gx // 2, 2, gy // 2)


def lookup(classes, entries):
    onehot = (classes[..., None] == jnp.arange(entries.shape[0], dtype=jnp.int32)).astype(
        jnp.float32
    )
    return jnp.sum(onehot * entries, axis=-1)


def edge_weights(padded):
    centre = padded[1:-1, 1:-1]
    north_w = 0.5 * (centre + padded[:-2, 1:-1])
    south_w = 0.5 * (centre + padded[2:, 1:-1])
    west_w = 0.5 * (centre + padded[1:-1, :-2])
    east_w = 0.5 * (centre + padded[1:-1, 2:])
    return (north_w, south_w, west_w, east_w)


def local(operator_t, data_columns, noise_var, class_map, diffusion_table, kappa_table):
    tile_rows, tile_cols, data_rows = operator_t.shape
    count, width = data_columns.shape
    gx_size, gy_size = lax.axis_size("gx"), lax.axis_size("gy")
    flattened = operator_t.reshape(tile_rows * tile_cols, data_rows)
    points = tile_rows * tile_cols
    extra = -(-points // width)
    classes = jnp.pad(class_map.reshape(points).astype(jnp.bfloat16), (0, extra * width - points))
    block = jnp.concatenate([data_columns, classes.reshape(extra, width)], axis=0)
    full = gather(mesh_dims(), block)
    data = full[..., :count, :].reshape(data_rows, width)
    classes = full[..., count:, :].reshape(gx_size, gy_size, extra * width)[..., :points]
    classes = classes.reshape(gx_size, gy_size, tile_rows, tile_cols).astype(jnp.int32)
    classes = classes.transpose(0, 2, 1, 3).reshape(gx_size * tile_rows, gy_size * tile_cols)
    edge = ITERS + 1
    classes = jnp.pad(classes, edge, constant_values=-1)
    window = lax.dynamic_slice(
        classes,
        (lax.axis_index("gx") * tile_rows, lax.axis_index("gy") * tile_cols),
        (tile_rows + 2 * edge, tile_cols + 2 * edge),
    )
    inside = (window >= 0)[1:-1, 1:-1]
    weights = edge_weights(lookup(window, diffusion_table))
    reaction = lookup(window, kappa_table)[1:-1, 1:-1]
    divisor = jnp.where(inside, reaction + weights[0] + weights[1] + weights[2] + weights[3], 1.0)
    coef = jnp.stack([jnp.where(inside, w / divisor, 0.0) for w in weights])
    coef = jnp.broadcast_to(coef[..., None], coef.shape + (128,))
    source = jnp.dot(flattened, data, preferred_element_type=jnp.float32)
    tile_divisor = divisor[ITERS:-ITERS, ITERS:-ITERS]
    start = source.reshape(tile_rows, tile_cols, width) / tile_divisor[..., None]
    iterate, smooth = smoothed(start, coef)
    forward = scatter(mesh_dims(), flattened, smooth.reshape(points, width), count)
    return (forward + noise_var[:, None] * data_columns.astype(jnp.float32), iterate)


def solution(mesh):
    placed = (P("gx", "gy", None), P(("gx", "gy"), None), P(("gx", "gy")), P("gx", "gy"), P(), P())
    return jax.shard_map(
        local,
        mesh=mesh,
        in_specs=placed,
        out_specs=(P(("gx", "gy"), None), P("gx", "gy", None)),
        check_vma=False,
    )
```

```python
import functools
import jax
import jax.numpy as jnp
from jax import lax
from jax.experimental import pallas as pl
from jax.experimental.pallas import tpu as pltpu
from jax.sharding import PartitionSpec as P

ITERS = 8
MESH = pl.DeviceIdType.MESH


def up8(n):
    return -(-n // 8) * 8


class Place:
    def __init__(self, dims):
        self.Y, self.X, self.Z = dims
        gx, gy = lax.axis_index("gx"), lax.axis_index("gy")
        self.y, self.x = gx // self.X, gx % self.X
        self.z, self.core = gy // 2, gy % 2
        self.n = {"x": self.X, "y": self.Y, "z": self.Z}
        self.at = {"x": self.x, "y": self.y, "z": self.z}

    def device(self, **moved):
        c = {**self.at, "core": self.core, **moved}
        return (c["y"] * self.X + c["x"], c["z"] * 2 + c["core"])

    def ahead(self, axis, d):
        return (self.at[axis] + d) % self.n[axis]

    def peers(self):
        found = [self.device(core=1 - self.core)]
        for axis in "xyz":
            found += [self.device(**{axis: self.ahead(axis, d)}) for d in range(1, self.n[axis])]
        return found

    def barrier(self):
        ready = pltpu.get_barrier_semaphore()
        peers = self.peers()
        for peer in peers:
            pl.semaphore_signal(ready, inc=1, device_id=peer, device_id_type=MESH)
        pl.semaphore_wait(ready, len(peers))


def remote(src, dst, send, recv, device):
    return pltpu.make_async_remote_copy(
        src_ref=src, dst_ref=dst, send_sem=send, recv_sem=recv, device_id=device, device_id_type=MESH
    )


def gather_kernel(dims, mine, full, own_sem, sz, rz, s1, r1, s2, r2, ss, rs):
    here = Place(dims)
    Y, X, Z = dims
    me = here.core
    sib = here.device(core=1 - me)
    home = full.at[here.y, here.x, here.z, me]
    copy = pltpu.make_async_copy(mine, home, own_sem)
    copy.start()
    here.barrier()
    copies = []
    for d in range(1, Z):
        sent = remote(mine, home, sz.at[d - 1], rz.at[d - 1], here.device(z=here.ahead("z", d)))
        sent.start()
        copies.append(sent)
    copy.wait()
    for c in (0, 1):

        @pl.when(me == c)
        def _():
            near, far = "xy"[c], "yx"[c]
            n1, n2 = here.n[near], here.n[far]
            sent_here = []

            def block(d, e, f, core):
                x, y = ((e, f), (f, e))[c]
                return full.at[here.ahead("y", -y), here.ahead("x", -x), here.ahead("z", -d), core]

            def share_number(d, e, f):
                x, y = ((e, f), (f, e))[c]
                return (d * X + x) * Y + y

            def start(*what):
                sent = remote(*what)
                sent.start()
                sent_here.append(sent)

            def arrived(ref, send, recv):
                remote(ref, ref, send, recv, sib).wait_recv()

            def to_far(held, d, e):
                for f in range(1, n2):
                    k = (d * n1 + e) * n2 + f
                    start(
                        held, held, s2.at[k], r2.at[k], here.device(**{far: here.ahead(far, f)})
                    )

            def to_sibling(held, d, e, f):
                k = share_number(d, e, f)
                start(held, held, ss.at[k], rs.at[k], sib)

            for d in range(Z):
                held = block(d, 0, 0, c)
                if d:
                    arrived(held, sz.at[d - 1], rz.at[d - 1])
                for e in range(1, n1):
                    k = d * n1 + e
                    start(
                        held, held, s1.at[k], r1.at[k], here.device(**{near: here.ahead(near, e)})
                    )
                to_far(held, d, 0)
                to_sibling(held, d, 0, 0)
            for d in range(Z):
                for e in range(1, n1):
                    held = block(d, e, 0, c)
                    arrived(held, s1.at[d * n1 + e], r1.at[d * n1 + e])
                    to_far(held, d, e)
                    to_sibling(held, d, e, 0)
            for e in range(n1):
                for d in range(Z):
                    for f in range(1, n2):
                        held = block(d, e, f, c)
                        k = (d * n1 + e) * n2 + f
                        arrived(held, s2.at[k], r2.at[k])
                        to_sibling(held, d, e, f)
            for d in range(Z):
                for e in range(n1):
                    for f in range(n2):
                        k = share_number(d, e, f)
                        arrived(block(d, e, f, 1 - c), ss.at[k], rs.at[k])
            for sent in sent_here:
                sent.wait_send()

    for sent in copies:
        sent.wait_send()


def gather(dims, block):
    Y, X, Z = dims
    dma = pltpu.SemaphoreType.DMA
    widest = max(X, Y)
    return pl.pallas_call(
        functools.partial(gather_kernel, dims),
        out_shape=jax.ShapeDtypeStruct((Y, X, Z, 2) + block.shape, block.dtype),
        in_specs=[pl.BlockSpec(memory_space=pltpu.VMEM)],
        out_specs=pl.BlockSpec(memory_space=pltpu.VMEM),
        scratch_shapes=[dma]
        + [dma((max(Z - 1, 1),))] * 2
        + [dma((Z * widest,))] * 2
        + [dma((X * Y * Z,))] * 4,
        compiler_params=pltpu.CompilerParams(
            collective_id=0, has_side_effects=True, vmem_limit_bytes=16 << 20
        ),
    )(block)


def scatter_kernel(dims, starts, H, fused, *refs):
    if fused:
        operator, field, out, total, r0, r1x, r1y, r2x, r2y, r3, part, wide, *sems = refs
    else:
        part, out, total, r0, r1x, r1y, r2x, r2y, r3, *sems = refs
    here = Place(dims)
    Y, X, Z = dims
    pair = part.shape[3]
    me = here.core
    sib = here.device(core=1 - me)
    s0, g0, s1, g1, s2, g2, s3, g3 = sems
    ready = pltpu.get_barrier_semaphore()
    peers = here.peers()
    for peer in peers:
        pl.semaphore_signal(ready, inc=1, device_id=peer, device_id_type=MESH)
    order = [(dy, dx) for dy in [*range(1, Y), 0] for dx in [*range(1, X), 0]]
    order.sort(key=lambda step: (step[0] == 0) + (step[1] == 0))
    for number, (dy, dx) in enumerate(order):
        y, x = here.ahead("y", dy), here.ahead("x", dx)
        if fused:
            span = wide.shape[0]
            row = (y * X + x) * (Z * pair)
            base = jnp.minimum(row // 128, (operator.shape[1] - span) // 128) * 128
            wide[...] = lax.dot_general(
                operator[:, pl.ds(pl.multiple_of(base, 128), span)],
                field[...],
                (((0,), (0,)), ((), ())),
                preferred_element_type=jnp.float32,
            )
            for z in range(Z):
                part[y, x, z] = wide[pl.ds(pl.multiple_of(row - base + z * pair, 8), pair), :]
        if number == 0:
            pl.semaphore_wait(ready, len(peers))
        for c in (0, 1):

            @pl.when(me == c)
            def _():
                remote(
                    part.at[y, x, :, pl.ds(starts[1 - c], H), :],
                    r0.at[y, x],
                    s0.at[number],
                    g0.at[number],
                    sib,
                ).start()

    for c in (0, 1):

        @pl.when(me == c)
        def _():
            near, far = "xy"[c], "yx"[c]
            r1, r2 = (r1x, r2y) if c == 0 else (r1y, r2x)
            n1, n2 = here.n[near], here.n[far]
            sent_here = []
            sorted_steps = sorted(
                enumerate(order), key=lambda item: (item[1][1 - c] == 0, item[0])
            )
            for number, (dy, dx) in sorted_steps:
                y, x = here.ahead("y", dy), here.ahead("x", dx)
                arrived = r0.at[y, x]
                remote(arrived, arrived, s0.at[number], g0.at[number], sib).wait_recv()
                held = total.at[y, x]
                held[...] = part[y, x, :, pl.ds(starts[c], H), :] + arrived[...]
                d = (dx, dy)[c]
                if d:
                    sent = remote(
                        held,
                        r1.at[d - 1, (y, x)[c]],
                        s1.at[number],
                        g1.at[number],
                        here.device(**{near: (x, y)[c]}),
                    )
                    sent.start()
                    sent_here.append(sent)
            for d2 in [*range(1, n2), 0]:
                index = here.ahead(far, d2)
                held = total.at[(index, here.x) if c == 0 else (here.y, index)]
                value = held[...]
                for d in range(1, n1):
                    number = order.index((d2, d) if c == 0 else (d, d2))
                    back = r1.at[d - 1, index]
                    remote(back, back, s1.at[number], g1.at[number], sib).wait_recv()
                    value = value + back[...]
                held[...] = value
                if d2:
                    for d in [*range(1, Z), 0]:
                        z, k = here.ahead("z", d), (d2 - 1) * Z + d
                        sent = remote(
                            held.at[z], r2.at[d2 - 1, z], s2.at[k], g2.at[k],
                            here.device(**{far: index}),
                        )
                        sent.start()
                        sent_here.append(sent)
            for d in [*range(1, Z), 0]:
                index = here.ahead("z", d)
                held = total.at[here.y, here.x, index]
                value = held[...]
                for e in range(1, n2):
                    back, k = r2.at[e - 1, index], (e - 1) * Z + d
                    remote(back, back, s2.at[k], g2.at[k], sib).wait_recv()
                    value = value + back[...]
                held[...] = value
                if d:
                    sent = remote(
                        held, r3.at[d - 1], s3.at[d - 1], g3.at[d - 1], here.device(z=index)
                    )
                    sent.start()
                    sent_here.append(sent)
            value = total.at[here.y, here.x, here.z][...]
            for d in range(1, Z):
                remote(r3.at[d - 1], r3.at[d - 1], s3.at[d - 1], g3.at[d - 1], sib).wait_recv()
                value = value + r3.at[d - 1][...]
            out[...] = value
            for sent in sent_here:
                sent.wait_send()
            for number, (dy, dx) in enumerate(order):
                y, x = here.ahead("y", dy), here.ahead("x", dx)
                remote(
                    part.at[y, x, :, pl.ds(starts[1 - c], H), :],
                    r0.at[y, x],
                    s0.at[number],
                    g0.at[number],
                    sib,
                ).wait_send()


def scatter(dims, operator, field, rows):
    Y, X, Z = dims
    points, data_rows = operator.shape
    columns = field.shape[1]
    start = rows // 8 * 8
    H = max(up8(rows), up8(2 * rows) - start)
    pair = max(H + start, 2 * rows)
    group = Z * pair
    span = -(-(group + 127) // 128) * 128
    fused = pair == 2 * rows and pair % 8 == 0 and data_rows % 128 == 0 and span <= data_rows
    dma = pltpu.SemaphoreType.DMA
    widest = max(X, Y)
    f32 = jnp.float32

    def held(*lead):
        return pltpu.VMEM(tuple(max(n, 1) for n in lead) + (H, columns), f32)

    scratch = [
        held(Y, X, Z),
        held(Y, X, Z),
        held(X - 1, Y, Z),
        held(Y - 1, X, Z),
        held(X - 1, Z),
        held(Y - 1, Z),
        held(Z - 1),
    ]
    if fused:
        given = (operator, field)
        scratch += [pltpu.VMEM((Y, X, Z, pair, columns), f32), pltpu.VMEM((span, columns), f32)]
    else:
        part = lax.dot_general(
            operator, field, (((0,), (0,)), ((), ())), preferred_element_type=f32
        ).reshape(Y, X, Z, 2 * rows, columns)
        given = (jnp.pad(part, ((0, 0),) * 3 + ((0, pair - 2 * rows), (0, 0))),)
    vmem = pl.BlockSpec(memory_space=pltpu.VMEM)
    out = pl.pallas_call(
        functools.partial(scatter_kernel, dims, (0, start), H, fused),
        out_shape=jax.ShapeDtypeStruct((H, columns), f32),
        in_specs=[vmem] * len(given),
        out_specs=vmem,
        scratch_shapes=scratch
        + [dma((X * Y,))] * 4
        + [dma((widest * Z,))] * 2
        + [dma((max(Z - 1, 1),))] * 2,
        compiler_params=pltpu.CompilerParams(
            collective_id=1, has_side_effects=True, vmem_limit_bytes=40 << 20
        ),
    )(*given)
    core = lax.axis_index("gy") % 2
    return jnp.where(core == 0, out[:rows], out[rows - start : 2 * rows - start])


def smooth_kernel(
    counts, start, coef, prior, smooth, s, u, v, up_out, down_out, up_in, down_in, local, send, recv
):
    rows, cols, width = start.shape
    m = ITERS
    gx, gy = lax.axis_index("gx"), lax.axis_index("gy")
    count_x, count_y = counts
    sides = {
        "n": (gx > 0, (gx - 1, gy), gx < count_x - 1),
        "s": (gx < count_x - 1, (gx + 1, gy), gx > 0),
        "w": (gy > 0, (gx, gy - 1), gy < count_y - 1),
        "e": (gy < count_y - 1, (gx, gy + 1), gy > 0),
    }
    inner_r, inner_c = pl.ds(m, rows), pl.ds(m, cols)
    low, high_r, high_c = pl.ds(0, m), pl.ds(m + rows, m), pl.ds(m + cols, m)
    home = pltpu.make_async_copy(start, s.at[inner_r, inner_c], local)
    home.start()
    for side, where in (("n", (low, slice(None))), ("s", (high_r, slice(None)))):

        @pl.when(jnp.logical_not(sides[side][0]))
        def _():
            s[where] = jnp.zeros((m, cols + 2 * m, width), jnp.float32)

    for side, where in (("w", low), ("e", high_c)):

        @pl.when(jnp.logical_not(sides[side][0]))
        def _():
            s[:, where] = jnp.zeros((rows + 2 * m, m, width), jnp.float32)

    ready = pltpu.get_barrier_semaphore()
    for has, peer, _ in sides.values():

        @pl.when(has)
        def _():
            pl.semaphore_signal(ready, inc=1, device_id=peer, device_id_type=MESH)

    up_out[...] = start[1:m].astype(jnp.bfloat16)
    down_out[...] = start[rows - m : rows - 1].astype(jnp.bfloat16)
    pl.semaphore_wait(ready, sum(jnp.where(has, 1, 0) for has, _, _ in sides.values()))

    first = (
        (0, "n", start.at[pl.ds(0, 1)], s.at[pl.ds(m + rows, 1), inner_c]),
        (1, "s", start.at[pl.ds(rows - 1, 1)], s.at[pl.ds(m - 1, 1), inner_c]),
        (2, "n", up_out, up_in),
        (3, "s", down_out, down_in),
        (4, "w", start.at[:, pl.ds(0, m)], s.at[inner_r, high_c]),
        (5, "e", start.at[:, pl.ds(cols - m, m)], s.at[inner_r, low]),
    )
    second = (
        (6, "w", s.at[low, pl.ds(m, m)], s.at[low, high_c]),
        (7, "w", s.at[high_r, pl.ds(m, m)], s.at[high_r, high_c]),
        (8, "e", s.at[low, pl.ds(cols, m)], s.at[low, low]),
        (9, "e", s.at[high_r, pl.ds(cols, m)], s.at[high_r, low]),
    )

    def each(group, what):
        for number, side, src, dst in group:
            has, peer, gets = sides[side]
            copy = remote(src, dst, send.at[number], recv.at[number], peer)

            @pl.when(gets if what == "wait_recv" else has)
            def _():
                getattr(copy, what)()

    each(first, "start")
    home.wait()
    each(first, "wait_recv")

    @pl.when(sides["s"][0])
    def _():
        s[pl.ds(m + rows + 1, m - 1), inner_c] = up_in[...].astype(jnp.float32)

    @pl.when(sides["n"][0])
    def _():
        s[pl.ds(0, m - 1), inner_c] = down_in[...].astype(jnp.float32)

    each(second, "start")
    each(second, "wait_recv")
    each(first, "wait_send")
    each(second, "wait_send")

    held = [s, u, v]
    wide = cols + 2 * m
    for step in range(1, ITERS + 1):
        old = s if step == 1 else held[1 + step % 2]
        new = held[1 + (step + 1) % 2]
        last = step == ITERS

        @pl.loop(step, rows + 2 * m - step)
        def _(r):
            for g in range(width // 128):
                lanes = pl.ds(g * 128, 128)
                centre = old[r, :, lanes]
                value = s[r, :, lanes] + coef[0, r] * old[r - 1, :, lanes]
                value = value + coef[1, r] * old[r + 1, :, lanes]
                value = value + coef[2, r] * pltpu.roll(centre, 1, 0)
                value = value + coef[3, r] * pltpu.roll(centre, wide - 1, 0)
                if last:
                    prior[r - m, :, lanes] = value[m : m + cols]
                    smooth[r - m, :, lanes] = value[m : m + cols].astype(jnp.bfloat16)
                else:
                    new[r, :, lanes] = value


def smoothed(start, coef):
    rows, cols, width = start.shape
    m = ITERS
    whole = pltpu.VMEM((rows + 2 * m, cols + 2 * m, width), jnp.float32)
    strip = pltpu.VMEM((m - 1, cols, width), jnp.bfloat16)
    dma = pltpu.SemaphoreType.DMA
    vmem = pl.BlockSpec(memory_space=pltpu.VMEM)
    return pl.pallas_call(
        functools.partial(smooth_kernel, (lax.axis_size("gx"), lax.axis_size("gy"))),
        out_shape=(
            jax.ShapeDtypeStruct(start.shape, jnp.float32),
            jax.ShapeDtypeStruct(start.shape, jnp.bfloat16),
        ),
        in_specs=[vmem, vmem],
        out_specs=(vmem, vmem),
        scratch_shapes=[whole] * 3 + [strip] * 4 + [dma, dma((10,)), dma((10,))],
        compiler_params=pltpu.CompilerParams(
            collective_id=2, has_side_effects=True, vmem_limit_bytes=40 << 20
        ),
    )(start, coef)


def mesh_dims():
    gx, gy = lax.axis_size("gx"), lax.axis_size("gy")
    return (gx // 2, 2, gy // 2)


def lookup(classes, entries):
    onehot = (classes[..., None] == jnp.arange(entries.shape[0], dtype=jnp.int32)).astype(
        jnp.float32
    )
    return jnp.sum(onehot * entries, axis=-1)


def edge_weights(padded):
    centre = padded[1:-1, 1:-1]
    north_w = 0.5 * (centre + padded[:-2, 1:-1])
    south_w = 0.5 * (centre + padded[2:, 1:-1])
    west_w = 0.5 * (centre + padded[1:-1, :-2])
    east_w = 0.5 * (centre + padded[1:-1, 2:])
    return (north_w, south_w, west_w, east_w)


def local(operator_t, data_columns, noise_var, class_map, diffusion_table, kappa_table):
    tile_rows, tile_cols, data_rows = operator_t.shape
    count, width = data_columns.shape
    gx_size, gy_size = lax.axis_size("gx"), lax.axis_size("gy")
    flattened = operator_t.reshape(tile_rows * tile_cols, data_rows)
    points = tile_rows * tile_cols
    extra = -(-points // width)
    classes = jnp.pad(class_map.reshape(points).astype(jnp.bfloat16), (0, extra * width - points))
    block = jnp.concatenate([data_columns, classes.reshape(extra, width)], axis=0)
    full = gather(mesh_dims(), block)
    data = full[..., :count, :].reshape(data_rows, width)
    classes = full[..., count:, :].reshape(gx_size, gy_size, extra * width)[..., :points]
    classes = classes.reshape(gx_size, gy_size, tile_rows, tile_cols).astype(jnp.int32)
    classes = classes.transpose(0, 2, 1, 3).reshape(gx_size * tile_rows, gy_size * tile_cols)
    edge = ITERS + 1
    classes = jnp.pad(classes, edge, constant_values=-1)
    window = lax.dynamic_slice(
        classes,
        (lax.axis_index("gx") * tile_rows, lax.axis_index("gy") * tile_cols),
        (tile_rows + 2 * edge, tile_cols + 2 * edge),
    )
    inside = (window >= 0)[1:-1, 1:-1]
    weights = edge_weights(lookup(window, diffusion_table))
    reaction = lookup(window, kappa_table)[1:-1, 1:-1]
    divisor = jnp.where(inside, reaction + weights[0] + weights[1] + weights[2] + weights[3], 1.0)
    coef = jnp.stack([jnp.where(inside, w / divisor, 0.0) for w in weights])
    coef = jnp.broadcast_to(coef[..., None], coef.shape + (128,))
    source = jnp.dot(flattened, data, preferred_element_type=jnp.float32)
    tile_divisor = divisor[ITERS:-ITERS, ITERS:-ITERS]
    start = source.reshape(tile_rows, tile_cols, width) / tile_divisor[..., None]
    iterate, smooth = smoothed(start, coef)
    forward = scatter(mesh_dims(), flattened, smooth.reshape(points, width), count)
    return (forward + noise_var[:, None] * data_columns.astype(jnp.float32), iterate)


def solution(mesh):
    placed = (P("gx", "gy", None), P(("gx", "gy"), None), P(("gx", "gy")), P("gx", "gy"), P(), P())
    return jax.shard_map(
        local,
        mesh=mesh,
        in_specs=placed,
        out_specs=(P(("gx", "gy"), None), P("gx", "gy", None)),
        check_vma=False,
    )
```

```python
import functools
import jax
import jax.numpy as jnp
from jax import lax
from jax.experimental import pallas as pl
from jax.experimental.pallas import tpu as pltpu
from jax.sharding import PartitionSpec as P

ITERS = 8
MESH = pl.DeviceIdType.MESH


def up8(n):
    return -(-n // 8) * 8


class Place:
    def __init__(self, dims):
        self.Y, self.X, self.Z = dims
        gx, gy = lax.axis_index("gx"), lax.axis_index("gy")
        self.y, self.x = gx // self.X, gx % self.X
        self.z, self.core = gy // 2, gy % 2
        self.n = {"x": self.X, "y": self.Y, "z": self.Z}
        self.at = {"x": self.x, "y": self.y, "z": self.z}

    def device(self, **moved):
        c = {**self.at, "core": self.core, **moved}
        return (c["y"] * self.X + c["x"], c["z"] * 2 + c["core"])

    def ahead(self, axis, d):
        return (self.at[axis] + d) % self.n[axis]

    def peers(self):
        found = [self.device(core=1 - self.core)]
        for axis in "xyz":
            found += [self.device(**{axis: self.ahead(axis, d)}) for d in range(1, self.n[axis])]
        return found

    def barrier(self):
        ready = pltpu.get_barrier_semaphore()
        peers = self.peers()
        for peer in peers:
            pl.semaphore_signal(ready, inc=1, device_id=peer, device_id_type=MESH)
        pl.semaphore_wait(ready, len(peers))


def remote(src, dst, send, recv, device):
    return pltpu.make_async_remote_copy(
        src_ref=src, dst_ref=dst, send_sem=send, recv_sem=recv, device_id=device, device_id_type=MESH
    )


def gather_kernel(dims, mine, full, own_sem, sz, rz, s1, r1, s2, r2, ss, rs):
    here = Place(dims)
    Y, X, Z = dims
    me = here.core
    sib = here.device(core=1 - me)
    home = full.at[here.y, here.x, here.z, me]
    copy = pltpu.make_async_copy(mine, home, own_sem)
    copy.start()
    here.barrier()
    copies = []
    for d in range(1, Z):
        sent = remote(mine, home, sz.at[d - 1], rz.at[d - 1], here.device(z=here.ahead("z", d)))
        sent.start()
        copies.append(sent)
    copy.wait()
    for c in (0, 1):

        @pl.when(me == c)
        def _():
            near, far = "xy"[c], "yx"[c]
            n1, n2 = here.n[near], here.n[far]
            sent_here = []

            def block(d, e, f, core):
                x, y = ((e, f), (f, e))[c]
                return full.at[here.ahead("y", -y), here.ahead("x", -x), here.ahead("z", -d), core]

            def share_number(d, e, f):
                x, y = ((e, f), (f, e))[c]
                return (d * X + x) * Y + y

            def start(*what):
                sent = remote(*what)
                sent.start()
                sent_here.append(sent)

            def arrived(ref, send, recv):
                remote(ref, ref, send, recv, sib).wait_recv()

            def to_far(held, d, e):
                for f in range(1, n2):
                    k = (d * n1 + e) * n2 + f
                    start(
                        held, held, s2.at[k], r2.at[k], here.device(**{far: here.ahead(far, f)})
                    )

            def to_sibling(held, d, e, f):
                k = share_number(d, e, f)
                start(held, held, ss.at[k], rs.at[k], sib)

            for d in range(Z):
                held = block(d, 0, 0, c)
                if d:
                    arrived(held, sz.at[d - 1], rz.at[d - 1])
                for e in range(1, n1):
                    k = d * n1 + e
                    start(
                        held, held, s1.at[k], r1.at[k], here.device(**{near: here.ahead(near, e)})
                    )
                to_far(held, d, 0)
                to_sibling(held, d, 0, 0)
            for d in range(Z):
                for e in range(1, n1):
                    held = block(d, e, 0, c)
                    arrived(held, s1.at[d * n1 + e], r1.at[d * n1 + e])
                    to_far(held, d, e)
                    to_sibling(held, d, e, 0)
            for e in range(n1):
                for d in range(Z):
                    for f in range(1, n2):
                        held = block(d, e, f, c)
                        k = (d * n1 + e) * n2 + f
                        arrived(held, s2.at[k], r2.at[k])
                        to_sibling(held, d, e, f)
            for d in range(Z):
                for e in range(n1):
                    for f in range(n2):
                        k = share_number(d, e, f)
                        arrived(block(d, e, f, 1 - c), ss.at[k], rs.at[k])
            for sent in sent_here:
                sent.wait_send()

    for sent in copies:
        sent.wait_send()


def gather(dims, block):
    Y, X, Z = dims
    dma = pltpu.SemaphoreType.DMA
    widest = max(X, Y)
    return pl.pallas_call(
        functools.partial(gather_kernel, dims),
        out_shape=jax.ShapeDtypeStruct((Y, X, Z, 2) + block.shape, block.dtype),
        in_specs=[pl.BlockSpec(memory_space=pltpu.VMEM)],
        out_specs=pl.BlockSpec(memory_space=pltpu.VMEM),
        scratch_shapes=[dma]
        + [dma((max(Z - 1, 1),))] * 2
        + [dma((Z * widest,))] * 2
        + [dma((X * Y * Z,))] * 4,
        compiler_params=pltpu.CompilerParams(
            collective_id=0, has_side_effects=True, vmem_limit_bytes=16 << 20
        ),
    )(block)


def scatter_kernel(dims, starts, H, fused, *refs):
    if fused:
        operator, field, out, total, r0, r1x, r1y, r2x, r2y, r3, part, wide, *sems = refs
    else:
        part, out, total, r0, r1x, r1y, r2x, r2y, r3, *sems = refs
    here = Place(dims)
    Y, X, Z = dims
    pair = part.shape[3]
    me = here.core
    sib = here.device(core=1 - me)
    s0, g0, s1, g1, s2, g2, s3, g3 = sems
    ready = pltpu.get_barrier_semaphore()
    peers = here.peers()
    for peer in peers:
        pl.semaphore_signal(ready, inc=1, device_id=peer, device_id_type=MESH)
    order = [(dy, dx) for dy in [*range(1, Y), 0] for dx in [*range(1, X), 0]]
    order.sort(key=lambda step: (step[0] == 0) + (step[1] == 0))
    for number, (dy, dx) in enumerate(order):
        y, x = here.ahead("y", dy), here.ahead("x", dx)
        if fused:
            span = wide.shape[0]
            row = (y * X + x) * (Z * pair)
            base = jnp.minimum(row // 128, (operator.shape[1] - span) // 128) * 128
            wide[...] = lax.dot_general(
                operator[:, pl.ds(pl.multiple_of(base, 128), span)],
                field[...],
                (((0,), (0,)), ((), ())),
                preferred_element_type=jnp.float32,
            )
            for z in range(Z):
                part[y, x, z] = wide[pl.ds(pl.multiple_of(row - base + z * pair, 8), pair), :]
        if number == 0:
            pl.semaphore_wait(ready, len(peers))
        for c in (0, 1):

            @pl.when(me == c)
            def _():
                remote(
                    part.at[y, x, :, pl.ds(starts[1 - c], H), :],
                    r0.at[y, x],
                    s0.at[number],
                    g0.at[number],
                    sib,
                ).start()

    for c in (0, 1):

        @pl.when(me == c)
        def _():
            near, far = "xy"[c], "yx"[c]
            r1, r2 = (r1x, r2y) if c == 0 else (r1y, r2x)
            n1, n2 = here.n[near], here.n[far]
            sent_here = []
            sorted_steps = sorted(
                enumerate(order), key=lambda item: (item[1][1 - c] == 0, item[0])
            )
            for number, (dy, dx) in sorted_steps:
                y, x = here.ahead("y", dy), here.ahead("x", dx)
                arrived = r0.at[y, x]
                remote(arrived, arrived, s0.at[number], g0.at[number], sib).wait_recv()
                held = total.at[y, x]
                held[...] = part[y, x, :, pl.ds(starts[c], H), :] + arrived[...]
                d = (dx, dy)[c]
                if d:
                    for dz in [*range(1, Z), 0]:
                        z, k = here.ahead("z", dz), number * Z + dz
                        sent = remote(
                            held.at[z],
                            r1.at[d - 1, (y, x)[c], z],
                            s1.at[k],
                            g1.at[k],
                            here.device(**{near: (x, y)[c]}),
                        )
                        sent.start()
                        sent_here.append(sent)
            for d2 in [*range(1, n2), 0]:
                index = here.ahead(far, d2)
                held = total.at[(index, here.x) if c == 0 else (here.y, index)]
                for dz in [*range(1, Z), 0]:
                    z = here.ahead("z", dz)
                    value = held[z]
                    for d in range(1, n1):
                        k = order.index((d2, d) if c == 0 else (d, d2)) * Z + dz
                        back = r1.at[d - 1, index, z]
                        remote(back, back, s1.at[k], g1.at[k], sib).wait_recv()
                        value = value + back[...]
                    held[z] = value
                    if d2:
                        k = (d2 - 1) * Z + dz
                        sent = remote(
                            held.at[z], r2.at[d2 - 1, z], s2.at[k], g2.at[k],
                            here.device(**{far: index}),
                        )
                        sent.start()
                        sent_here.append(sent)
            for d in [*range(1, Z), 0]:
                index = here.ahead("z", d)
                held = total.at[here.y, here.x, index]
                value = held[...]
                for e in range(1, n2):
                    back, k = r2.at[e - 1, index], (e - 1) * Z + d
                    remote(back, back, s2.at[k], g2.at[k], sib).wait_recv()
                    value = value + back[...]
                held[...] = value
                if d:
                    sent = remote(
                        held, r3.at[d - 1], s3.at[d - 1], g3.at[d - 1], here.device(z=index)
                    )
                    sent.start()
                    sent_here.append(sent)
            value = total.at[here.y, here.x, here.z][...]
            for d in range(1, Z):
                remote(r3.at[d - 1], r3.at[d - 1], s3.at[d - 1], g3.at[d - 1], sib).wait_recv()
                value = value + r3.at[d - 1][...]
            out[...] = value
            for sent in sent_here:
                sent.wait_send()
            for number, (dy, dx) in enumerate(order):
                y, x = here.ahead("y", dy), here.ahead("x", dx)
                remote(
                    part.at[y, x, :, pl.ds(starts[1 - c], H), :],
                    r0.at[y, x],
                    s0.at[number],
                    g0.at[number],
                    sib,
                ).wait_send()


def scatter(dims, operator, field, rows):
    Y, X, Z = dims
    points, data_rows = operator.shape
    columns = field.shape[1]
    start = rows // 8 * 8
    H = max(up8(rows), up8(2 * rows) - start)
    pair = max(H + start, 2 * rows)
    group = Z * pair
    span = -(-(group + 127) // 128) * 128
    fused = pair == 2 * rows and pair % 8 == 0 and data_rows % 128 == 0 and span <= data_rows
    dma = pltpu.SemaphoreType.DMA
    widest = max(X, Y)
    f32 = jnp.float32

    def held(*lead):
        return pltpu.VMEM(tuple(max(n, 1) for n in lead) + (H, columns), f32)

    scratch = [
        held(Y, X, Z),
        held(Y, X, Z),
        held(X - 1, Y, Z),
        held(Y - 1, X, Z),
        held(X - 1, Z),
        held(Y - 1, Z),
        held(Z - 1),
    ]
    if fused:
        given = (operator, field)
        scratch += [pltpu.VMEM((Y, X, Z, pair, columns), f32), pltpu.VMEM((span, columns), f32)]
    else:
        part = lax.dot_general(
            operator, field, (((0,), (0,)), ((), ())), preferred_element_type=f32
        ).reshape(Y, X, Z, 2 * rows, columns)
        given = (jnp.pad(part, ((0, 0),) * 3 + ((0, pair - 2 * rows), (0, 0))),)
    vmem = pl.BlockSpec(memory_space=pltpu.VMEM)
    out = pl.pallas_call(
        functools.partial(scatter_kernel, dims, (0, start), H, fused),
        out_shape=jax.ShapeDtypeStruct((H, columns), f32),
        in_specs=[vmem] * len(given),
        out_specs=vmem,
        scratch_shapes=scratch
        + [dma((X * Y * Z,))] * 4
        + [dma((widest * Z,))] * 2
        + [dma((max(Z - 1, 1),))] * 2,
        compiler_params=pltpu.CompilerParams(
            collective_id=1, has_side_effects=True, vmem_limit_bytes=40 << 20
        ),
    )(*given)
    core = lax.axis_index("gy") % 2
    return jnp.where(core == 0, out[:rows], out[rows - start : 2 * rows - start])


def smooth_kernel(
    counts, start, coef, prior, smooth, s, u, v, up_out, down_out, up_in, down_in, local, send, recv
):
    rows, cols, width = start.shape
    m = ITERS
    gx, gy = lax.axis_index("gx"), lax.axis_index("gy")
    count_x, count_y = counts
    sides = {
        "n": (gx > 0, (gx - 1, gy), gx < count_x - 1),
        "s": (gx < count_x - 1, (gx + 1, gy), gx > 0),
        "w": (gy > 0, (gx, gy - 1), gy < count_y - 1),
        "e": (gy < count_y - 1, (gx, gy + 1), gy > 0),
    }
    inner_r, inner_c = pl.ds(m, rows), pl.ds(m, cols)
    low, high_r, high_c = pl.ds(0, m), pl.ds(m + rows, m), pl.ds(m + cols, m)
    home = pltpu.make_async_copy(start, s.at[inner_r, inner_c], local)
    home.start()
    for side, where in (("n", (low, slice(None))), ("s", (high_r, slice(None)))):

        @pl.when(jnp.logical_not(sides[side][0]))
        def _():
            s[where] = jnp.zeros((m, cols + 2 * m, width), jnp.float32)

    for side, where in (("w", low), ("e", high_c)):

        @pl.when(jnp.logical_not(sides[side][0]))
        def _():
            s[:, where] = jnp.zeros((rows + 2 * m, m, width), jnp.float32)

    ready = pltpu.get_barrier_semaphore()
    for has, peer, _ in sides.values():

        @pl.when(has)
        def _():
            pl.semaphore_signal(ready, inc=1, device_id=peer, device_id_type=MESH)

    up_out[...] = start[1:m].astype(jnp.bfloat16)
    down_out[...] = start[rows - m : rows - 1].astype(jnp.bfloat16)
    pl.semaphore_wait(ready, sum(jnp.where(has, 1, 0) for has, _, _ in sides.values()))

    first = (
        (0, "n", start.at[pl.ds(0, 1)], s.at[pl.ds(m + rows, 1), inner_c]),
        (1, "s", start.at[pl.ds(rows - 1, 1)], s.at[pl.ds(m - 1, 1), inner_c]),
        (2, "n", up_out, up_in),
        (3, "s", down_out, down_in),
        (4, "w", start.at[:, pl.ds(0, m)], s.at[inner_r, high_c]),
        (5, "e", start.at[:, pl.ds(cols - m, m)], s.at[inner_r, low]),
    )
    second = (
        (6, "w", s.at[low, pl.ds(m, m)], s.at[low, high_c]),
        (7, "w", s.at[high_r, pl.ds(m, m)], s.at[high_r, high_c]),
        (8, "e", s.at[low, pl.ds(cols, m)], s.at[low, low]),
        (9, "e", s.at[high_r, pl.ds(cols, m)], s.at[high_r, low]),
    )

    def each(group, what):
        for number, side, src, dst in group:
            has, peer, gets = sides[side]
            copy = remote(src, dst, send.at[number], recv.at[number], peer)

            @pl.when(gets if what == "wait_recv" else has)
            def _():
                getattr(copy, what)()

    each(first, "start")
    home.wait()
    each(first, "wait_recv")

    @pl.when(sides["s"][0])
    def _():
        s[pl.ds(m + rows + 1, m - 1), inner_c] = up_in[...].astype(jnp.float32)

    @pl.when(sides["n"][0])
    def _():
        s[pl.ds(0, m - 1), inner_c] = down_in[...].astype(jnp.float32)

    each(second, "start")
    each(second, "wait_recv")
    each(first, "wait_send")
    each(second, "wait_send")

    held = [s, u, v]
    wide = cols + 2 * m
    for step in range(1, ITERS + 1):
        old = s if step == 1 else held[1 + step % 2]
        new = held[1 + (step + 1) % 2]
        last = step == ITERS

        @pl.loop(step, rows + 2 * m - step)
        def _(r):
            for g in range(width // 128):
                lanes = pl.ds(g * 128, 128)
                centre = old[r, :, lanes]
                value = s[r, :, lanes] + coef[0, r] * old[r - 1, :, lanes]
                value = value + coef[1, r] * old[r + 1, :, lanes]
                value = value + coef[2, r] * pltpu.roll(centre, 1, 0)
                value = value + coef[3, r] * pltpu.roll(centre, wide - 1, 0)
                if last:
                    prior[r - m, :, lanes] = value[m : m + cols]
                    smooth[r - m, :, lanes] = value[m : m + cols].astype(jnp.bfloat16)
                else:
                    new[r, :, lanes] = value


def smoothed(start, coef):
    rows, cols, width = start.shape
    m = ITERS
    whole = pltpu.VMEM((rows + 2 * m, cols + 2 * m, width), jnp.float32)
    strip = pltpu.VMEM((m - 1, cols, width), jnp.bfloat16)
    dma = pltpu.SemaphoreType.DMA
    vmem = pl.BlockSpec(memory_space=pltpu.VMEM)
    return pl.pallas_call(
        functools.partial(smooth_kernel, (lax.axis_size("gx"), lax.axis_size("gy"))),
        out_shape=(
            jax.ShapeDtypeStruct(start.shape, jnp.float32),
            jax.ShapeDtypeStruct(start.shape, jnp.bfloat16),
        ),
        in_specs=[vmem, vmem],
        out_specs=(vmem, vmem),
        scratch_shapes=[whole] * 3 + [strip] * 4 + [dma, dma((10,)), dma((10,))],
        compiler_params=pltpu.CompilerParams(
            collective_id=2, has_side_effects=True, vmem_limit_bytes=40 << 20
        ),
    )(start, coef)


def mesh_dims():
    gx, gy = lax.axis_size("gx"), lax.axis_size("gy")
    return (gx // 2, 2, gy // 2)


def lookup(classes, entries):
    onehot = (classes[..., None] == jnp.arange(entries.shape[0], dtype=jnp.int32)).astype(
        jnp.float32
    )
    return jnp.sum(onehot * entries, axis=-1)


def edge_weights(padded):
    centre = padded[1:-1, 1:-1]
    north_w = 0.5 * (centre + padded[:-2, 1:-1])
    south_w = 0.5 * (centre + padded[2:, 1:-1])
    west_w = 0.5 * (centre + padded[1:-1, :-2])
    east_w = 0.5 * (centre + padded[1:-1, 2:])
    return (north_w, south_w, west_w, east_w)


def local(operator_t, data_columns, noise_var, class_map, diffusion_table, kappa_table):
    tile_rows, tile_cols, data_rows = operator_t.shape
    count, width = data_columns.shape
    gx_size, gy_size = lax.axis_size("gx"), lax.axis_size("gy")
    flattened = operator_t.reshape(tile_rows * tile_cols, data_rows)
    points = tile_rows * tile_cols
    extra = -(-points // width)
    classes = jnp.pad(class_map.reshape(points).astype(jnp.bfloat16), (0, extra * width - points))
    block = jnp.concatenate([data_columns, classes.reshape(extra, width)], axis=0)
    full = gather(mesh_dims(), block)
    data = full[..., :count, :].reshape(data_rows, width)
    classes = full[..., count:, :].reshape(gx_size, gy_size, extra * width)[..., :points]
    classes = classes.reshape(gx_size, gy_size, tile_rows, tile_cols).astype(jnp.int32)
    classes = classes.transpose(0, 2, 1, 3).reshape(gx_size * tile_rows, gy_size * tile_cols)
    edge = ITERS + 1
    classes = jnp.pad(classes, edge, constant_values=-1)
    window = lax.dynamic_slice(
        classes,
        (lax.axis_index("gx") * tile_rows, lax.axis_index("gy") * tile_cols),
        (tile_rows + 2 * edge, tile_cols + 2 * edge),
    )
    inside = (window >= 0)[1:-1, 1:-1]
    weights = edge_weights(lookup(window, diffusion_table))
    reaction = lookup(window, kappa_table)[1:-1, 1:-1]
    divisor = jnp.where(inside, reaction + weights[0] + weights[1] + weights[2] + weights[3], 1.0)
    coef = jnp.stack([jnp.where(inside, w / divisor, 0.0) for w in weights])
    coef = jnp.broadcast_to(coef[..., None], coef.shape + (128,))
    source = jnp.dot(flattened, data, preferred_element_type=jnp.float32)
    tile_divisor = divisor[ITERS:-ITERS, ITERS:-ITERS]
    start = source.reshape(tile_rows, tile_cols, width) / tile_divisor[..., None]
    iterate, smooth = smoothed(start, coef)
    forward = scatter(mesh_dims(), flattened, smooth.reshape(points, width), count)
    return (forward + noise_var[:, None] * data_columns.astype(jnp.float32), iterate)


def solution(mesh):
    placed = (P("gx", "gy", None), P(("gx", "gy"), None), P(("gx", "gy")), P("gx", "gy"), P(), P())
    return jax.shard_map(
        local,
        mesh=mesh,
        in_specs=placed,
        out_specs=(P(("gx", "gy"), None), P("gx", "gy", None)),
        check_vma=False,
    )
```
